768 devices in a mesh: dp: 96 (over y, z_lo, core), fsdp: 8 (over x, z_hi).
Axes of the slice: x: 4, y: 8, z: 12 (z_hi: 2, z_lo: 6; z = z_hi * 6 + z_lo), core: 2. Of those that a mesh axis runs over, the one named last changes fastest.
Arguments:
- query: bfloat16 [12288, 4096], P('dp', 'fsdp'), may hold values from -6 to 6
- key: bfloat16 [12288, 4096], P('dp', 'fsdp'), may hold values from -6 to 6
- value: bfloat16 [12288, 4096], P('dp', 'fsdp'), may hold values from -6 to 6
- upstream: bfloat16 [12288, 4096], P('dp', 'fsdp'), may hold values from -480 to 480
- reward: int32 [12288], P('dp'), may hold values from -4 to 4
- lengths: int32 [4], replicated, may hold values from 1 to 192, 384 in all
- se_filter: bfloat16 [3, 7, 4096], P(None, None, 'fsdp'), may hold values from -2 to 2
- mr_filter: bfloat16 [128, 256], P(None, 'fsdp'), may hold values from -0.5 to 0.5
Outputs:
- grad_se: float32 [3, 7, 4096], P(None, None, 'fsdp')
- grad_mr: float32 [128, 256], P(None, 'fsdp')
The draws below stay inside these ranges and needn't reach their ends.
Inputs may be any that keep to these rules, and one draw needn't show every extreme that they name: The sequence packs 4 whole documents in order; entry i is the length of document i in blocks of 32 tokens; the lengths sum to 384 and the longest is exactly 192. A token's reward weight is its level divided by 4.
All inputs are finite; a program needn't handle non-finite values.
Results may differ from the reference program's by a relative error of at most 0.0041.
Values may be sent and summed in bfloat16 or wider, within the bound.
A program may use at most 32 MiB of HBM per device.

```python
import math
import jax
import jax.numpy as jnp
import numpy as np
from jax import lax

CH = 4096
FGROUP = 16
GROUPS = 256
SELEN = 7
MRLEN = 128
BLOCK = 32
TOK_DEV = 128
NDOC = 4
SEQ = 12288
SEQ_BLOCKS = 384
N_FSDP = 8


def draw_upstream(key, part):
    first, second, third = jax.random.split(key, 3)
    rising = jnp.exp(jnp.log(3.0) * jnp.arange(CH, dtype=jnp.float32) / CH)
    channel_scale = rising * jnp.exp(jax.random.uniform(third, (CH,), jnp.float32, 0.0, jnp.log(4.0)))
    base = jnp.clip(jax.random.normal(first, (SEQ, CH), jnp.float32), -4.0, 4.0)
    row_scale = jnp.exp(jax.random.uniform(second, (SEQ, 1), jnp.float32, 0.0, jnp.log(10.0)))
    return (base * row_scale * channel_scale[None, :]).astype(jnp.bfloat16)


def with_ends(values, stream_key, smallest, top_value):
    longest = values.shape.index(max(values.shape))
    spots = []
    for shift in (0, 1):
        where = [jax.random.randint(jax.random.fold_in(stream_key, axis), (), 0, length) for axis, length in enumerate(values.shape)]
        where[longest] = (where[longest] + shift) % values.shape[longest]
        spots.append(tuple(where))
    return values.at[spots[0]].set(smallest).at[spots[1]].set(top_value)


def block_levels(own_key, shape, cuts, least, largest):
    level = 1.0
    for dim, shards_of in cuts:
        steps = jax.random.uniform(jax.random.fold_in(jax.random.fold_in(own_key, 6), dim), (shards_of,), jnp.float32, least / len(cuts), largest / len(cuts))
        level = level * jnp.repeat(jnp.exp(steps), shape[dim] // shards_of).reshape((-1,) + (1,) * (len(shape) - 1 - dim))
    return level


def length_profile(amount, total, limit, lean):
    portions = [(1 << 20) // math.isqrt(rank ** lean) + 1 for rank in range(2, amount + 1)]
    surplus, given = total - limit - (amount - 1), [1] * (amount - 1)
    while surplus > 0:
        movable = [i for i in range(amount - 1) if given[i] < limit]
        mass, left = sum([portions[i] for i in movable]), surplus
        for i in movable:
            more = min(limit - given[i], max(1, left * portions[i] // mass), surplus)
            given[i] = given[i] + more
            surplus = surplus - more
    return np.array([limit] + given)


def uneven_parts(rng, number_of, total, most, lean):
    if number_of == 2:
        one = jax.random.randint(rng, (), max(1, total - most), min(most, total - 1) + 1)
        return jnp.stack([one, total - one])
    sizes = jnp.asarray(length_profile(number_of, total, most, lean), jnp.int32)
    couples = (number_of - 1) // 2
    giver, taker = sizes[1:1 + 2 * couples:2], sizes[2:2 + 2 * couples:2]
    slack = jnp.minimum(giver - 1, most - taker)
    moved = jax.random.randint(jax.random.fold_in(rng, 1), (couples,), 0, 1 << 20) % (slack + 1)
    sizes = sizes.at[1:1 + 2 * couples:2].set(giver - moved).at[2:2 + 2 * couples:2].set(taker + moved)
    return sizes[jax.random.permutation(jax.random.fold_in(rng, 2), number_of)]


def noise(key, extent, scale, most, cuts=(), kind=jnp.bfloat16):
    values = jax.random.normal(key, extent, jnp.float32) * scale
    if len(cuts) > 0:
        values = block_levels(key, extent, cuts, -0.22, 0.18) * values
    return jnp.clip(values, min=-most, max=most).astype(kind)


def setup_inputs(seed: int = 0) -> dict:
    streams_of = jax.random.split(jax.random.key(seed), 9)
    query = noise(streams_of[0], (SEQ, CH), 1.0, 6.0, ((0, 96), (1, 8)))
    key = noise(streams_of[1], (SEQ, CH), 1.0, 6.0, ((0, 96), (1, 8)))
    value = noise(streams_of[2], (SEQ, CH), 1.0, 6.0, ((0, 96), (1, 8)))
    upstream = draw_upstream(jax.random.fold_in(streams_of[8], 71), 0)
    reward = with_ends(jax.random.randint(streams_of[4], (SEQ,), -4, 5), jax.random.fold_in(streams_of[4], 1), -4, 4).astype(jnp.int32)
    lengths = uneven_parts(streams_of[5], NDOC, SEQ_BLOCKS, SEQ_BLOCKS // 2, 1).astype(jnp.int32)
    se_filter = noise(streams_of[6], (3, SELEN, CH), SELEN ** -0.5, 2.0, ((2, 8),))
    mr_filter = noise(streams_of[7], (MRLEN, GROUPS), MRLEN ** -0.5, 0.5, ((1, 8),))
    return {"query": query, "key": key, "value": value, "upstream": upstream, "reward": reward, "lengths": lengths, "se_filter": se_filter, "mr_filter": mr_filter}


def block_docs(length_row, block_pos):
    ends = jnp.cumsum(length_row).astype(jnp.int32)
    counts = lax.optimization_barrier(jnp.sum((block_pos[:, None] >= ends[None, :]).astype(jnp.int32), axis=1)).astype(jnp.int32)
    return jnp.where(block_pos >= 0, counts, -1).astype(jnp.int32)

def band_matrix(vector, row_count):
    group_here, vec_len = vector.shape
    win_len = vec_len - 1
    tiled = jnp.tile(vector, (1, row_count))[:, :row_count * win_len]
    return tiled.reshape(group_here, row_count, win_len)

def forward_vector(medium_taps, block_rows):
    group_here = medium_taps.shape[1]
    head = jnp.zeros((group_here, 1), medium_taps.dtype)
    tail = jnp.zeros((group_here, block_rows), medium_taps.dtype)
    return jnp.concatenate([head, jnp.flip(medium_taps.T, axis=1), tail], axis=1)

def backward_vector(medium_taps, block_rows):
    group_here = medium_taps.shape[1]
    tail = jnp.zeros((group_here, block_rows + 1), medium_taps.dtype)
    return jnp.concatenate([medium_taps.T, tail], axis=1)

def diagonal_sums(products, filter_len):
    group_here, block_rows, win_len = products.shape
    flat = products.reshape(group_here, block_rows * win_len)
    flat = jnp.pad(flat, ((0, 0), (0, block_rows)))
    skewed = flat.reshape(group_here, block_rows, win_len + 1)
    totals = lax.optimization_barrier(jnp.sum(skewed[:, :, 1:filter_len + 1], axis=1))
    return jnp.flip(totals, axis=1).T

def block_windows(extended, sub_count, span_blocks, block_rows):
    channels = extended.shape[1]
    pieces = extended.reshape(sub_count + span_blocks, block_rows, channels)
    return jnp.stack([pieces[shift_idx:shift_idx + sub_count] for shift_idx in range(span_blocks + 1)], axis=1)

def short_filter(extended, token_docs, taps, row_count):
    edge = taps.shape[0] - 1
    result = jnp.zeros((row_count, extended.shape[1]), jnp.float32)
    for shift_idx in range(taps.shape[0]):
        begin = edge - shift_idx
        same_doc = (token_docs[edge:] == token_docs[begin:begin + row_count]).astype(jnp.float32)
        result = result + taps[shift_idx].astype(jnp.float32)[None, :] * extended[begin:begin + row_count].astype(jnp.float32) * same_doc[:, None]
    return result

def short_grads(cotangent, extended, token_docs, tap_count, row_count):
    edge = tap_count - 1
    rows_out = []
    for shift_idx in range(tap_count):
        begin = edge - shift_idx
        same_doc = (token_docs[edge:] == token_docs[begin:begin + row_count]).astype(jnp.float32)
        rows_out.append(lax.optimization_barrier(jnp.sum(cotangent * extended[begin:begin + row_count].astype(jnp.float32) * same_doc[:, None], axis=0)))
    return jnp.stack(rows_out, axis=0)

def reference(query, key, value, upstream, reward, lengths, se_filter, mr_filter):
    seq_rows = query.shape[0]
    slab_count = N_FSDP
    slab_width = CH // slab_count
    group_slab = GROUPS // slab_count
    block_rows = BLOCK
    filter_len = MRLEN
    edge = SELEN - 1
    sub_count = seq_rows // block_rows
    span_blocks = filter_len // block_rows
    win_len = block_rows + filter_len
    block_pos = jnp.arange(-span_blocks, sub_count + span_blocks, dtype=jnp.int32)
    docs_all = block_docs(lengths, block_pos)
    own_docs = docs_all[span_blocks:span_blocks + sub_count]
    fwd_mask = jnp.stack([own_docs == docs_all[idx:idx + sub_count] for idx in range(span_blocks + 1)], axis=1).astype(jnp.float32)
    bwd_mask = jnp.stack([own_docs == docs_all[span_blocks + idx:span_blocks + idx + sub_count] for idx in range(span_blocks + 1)], axis=1).astype(jnp.float32)
    token_docs = jnp.repeat(docs_all[span_blocks - 1:span_blocks + sub_count], block_rows)[block_rows - edge:]
    up_sq = lax.optimization_barrier(jnp.sum(jnp.square(upstream.astype(jnp.float32)), axis=1))
    inv_norm = lax.rsqrt(up_sq / CH + 1e-06)
    weight_rows = reward.astype(jnp.float32) * 0.25 * inv_norm

    def slabs(array):
        return jnp.transpose(array.reshape(seq_rows, slab_count, slab_width), (1, 0, 2))
    short_slabs = jnp.transpose(se_filter.reshape(3, SELEN, slab_count, slab_width), (2, 0, 1, 3))
    medium_slabs = jnp.transpose(mr_filter.reshape(MRLEN, slab_count, group_slab), (1, 0, 2))

    def per_slab(items):
        q_rows, k_rows, v_rows, up_rows, short_taps, medium_taps = items
        channels = q_rows.shape[1]
        group_all = medium_taps.shape[1]
        pad_rows = jnp.zeros((edge, channels), jnp.bfloat16)
        q_ext = jnp.concatenate([pad_rows, q_rows], axis=0)
        k_ext = jnp.concatenate([pad_rows, k_rows], axis=0)
        v_ext = jnp.concatenate([pad_rows, v_rows], axis=0)
        q_short = short_filter(q_ext, token_docs, short_taps[0], seq_rows)
        k_short = short_filter(k_ext, token_docs, short_taps[1], seq_rows)
        v_short = short_filter(v_ext, token_docs, short_taps[2], seq_rows)
        products = (k_short * v_short).astype(jnp.bfloat16)
        cotangent = weight_rows[:, None] * up_rows.astype(jnp.float32)
        dm_rows = (cotangent * q_short).astype(jnp.bfloat16)
        z_ext = jnp.concatenate([jnp.zeros((filter_len, channels), jnp.bfloat16), products], axis=0)
        z_win = block_windows(z_ext, sub_count, span_blocks, block_rows).astype(jnp.float32) * fwd_mask[:, :, None, None]
        z_win = z_win.reshape(sub_count, win_len, group_all, FGROUP)
        fwd_band = band_matrix(forward_vector(medium_taps, block_rows), block_rows).astype(jnp.float32)
        medium = jnp.einsum('gpr,nrgc->npgc', fwd_band, z_win, precision=lax.Precision.HIGHEST).reshape(seq_rows, channels)
        dm_ext = jnp.concatenate([dm_rows, jnp.zeros((filter_len, channels), jnp.bfloat16)], axis=0)
        dm_win = block_windows(dm_ext, sub_count, span_blocks, block_rows).astype(jnp.float32) * bwd_mask[:, :, None, None]
        dm_win = dm_win.reshape(sub_count, win_len, group_all, FGROUP)
        bwd_band = band_matrix(backward_vector(medium_taps, block_rows), block_rows).astype(jnp.float32)
        dz_rows = jnp.einsum('gpr,nrgc->npgc', bwd_band, dm_win, precision=lax.Precision.HIGHEST).reshape(seq_rows, channels)
        dm_four = dm_rows.astype(jnp.float32).reshape(sub_count, block_rows, group_all, FGROUP)
        pair = jnp.einsum('npgc,nrgc->gpr', dm_four, z_win, precision=lax.Precision.HIGHEST)
        grad_medium = diagonal_sums(pair, filter_len)
        cot_query = cotangent * medium
        cot_key = dz_rows * v_short
        cot_value = dz_rows * k_short
        grad_short = jnp.stack([short_grads(cot_query, q_ext, token_docs, SELEN, seq_rows), short_grads(cot_key, k_ext, token_docs, SELEN, seq_rows), short_grads(cot_value, v_ext, token_docs, SELEN, seq_rows)], axis=0)
        return (grad_short, grad_medium)
    short_all, medium_all = lax.map(per_slab, (slabs(query), slabs(key), slabs(value), slabs(upstream), short_slabs, medium_slabs))
    grad_se = jnp.transpose(short_all, (1, 2, 0, 3)).reshape(3, SELEN, CH)
    grad_mr = jnp.transpose(medium_all, (1, 0, 2)).reshape(MRLEN, GROUPS)
    return (grad_se / TOK_DEV, grad_mr / TOK_DEV)
```

```python
import jax
import jax.numpy as jnp
from jax import lax
from jax.experimental import pallas as pl
from jax.experimental.pallas import tpu as pltpu
from jax.sharding import PartitionSpec as P

MESH = pl.DeviceIdType.MESH
CH = 4096
ROWS = 128
COLS = 512
BLK = 32
NB = 4
TAPS = 7
GRP = 32
LANES = 128
NY, NZ, NX = 8, 6, 4
DP = 96
TEAM = 16

X0, ZP0, RIM0, ZH0, UH0, RS0, ZZ0, AG0, NSEM = 0, 3, 6, 9, 11, 13, 28, 33, 48


def main_kernel(
    q_hbm, k_hbm, v_hbm, u_hbm, rew_hbm, len_ref, se_hbm, mr_hbm, out_ref,
    raw, rewb, seb, mrb, rim, ext, short, zown, zprev, uqf, uqb, uqn, umb, mask, tf, tb, skew,
    xs, xr, zs, zr, scol, dmo, dmn, pay, rsb, zzb, fin, got,
    lsem, ssem, rsem,
):
    d = lax.axis_index("dp")
    f = lax.axis_index("fsdp")
    core = lax.rem(d, 2)
    zlo = lax.rem(d // 2, NZ)
    y = d // (2 * NZ)
    xx, zhi = f // 2, lax.rem(f, 2)
    nxt, prv = lax.rem(d + 1, DP), lax.rem(d + DP - 1, DP)
    me = y * 2 + core
    fz = xx * 2 + (1 - zhi)

    def x_peer(o):
        return (d, lax.rem(xx + o, NX) * 2 + zhi)

    def team_of(i):
        return ((i // 2) * (2 * NZ) + zlo * 2 + lax.rem(i, 2), f)

    def z_peer(o):
        return (y * (2 * NZ) + lax.rem(zlo + o, NZ) * 2 + core, f)

    peers = [x_peer(o) for o in range(1, NX)]
    peers += [(d, fz), (prv, f), (nxt, f), (prv, fz), (nxt, fz)]
    peers += [team_of(lax.rem(me + o, TEAM)) for o in range(1, TEAM)]
    peers += [z_peer(o) for o in range(1, NZ)]
    barrier = pltpu.get_barrier_semaphore()
    for dev in peers:
        pl.semaphore_signal(barrier, inc=1, device_id=dev, device_id_type=MESH)

    def send(src, dst, idx, dev):
        return pltpu.make_async_remote_copy(
            src_ref=src, dst_ref=dst, send_sem=ssem.at[idx], recv_sem=rsem.at[idx],
            device_id=dev, device_id_type=MESH,
        )

    loads = [
        pltpu.make_async_copy(src, dst, lsem.at[i])
        for i, (src, dst) in enumerate([
            (u_hbm, raw.at[3]), (k_hbm, raw.at[1]), (v_hbm, raw.at[2]), (q_hbm, raw.at[0]),
            (rew_hbm, rewb), (se_hbm, seb), (mr_hbm, mrb),
        ])
    ]
    for c in loads:
        c.start()

    ends = [len_ref[0]]
    for i in range(1, 4):
        ends.append(ends[-1] + len_ref[i])
    base = d * NB

    def doc(b):
        n = jnp.zeros_like(b)
        for e in ends:
            n = n + (b >= e).astype(jnp.int32)
        return jnp.where(b < 0, -1, n)

    ri = lax.broadcasted_iota(jnp.int32, (ROWS, LANES), 0)
    ci = lax.broadcasted_iota(jnp.int32, (ROWS, LANES), 1)
    cr = (LANES - 1) - ci
    own_row = doc(base + (ri >> 5))
    own_col = doc(base + (ci >> 5))

    def put_mask(i, cond, a, b):
        mask[i] = jnp.where(cond & (a == b), 1.0, 0.0).astype(jnp.float32)

    put_mask(0, ci > ri, own_row, doc(base - NB + (ci >> 5)))
    put_mask(1, ci <= ri, own_row, own_col)
    put_mask(2, ci < ri, own_row, doc(base + NB + (ci >> 5)))
    put_mask(3, ci >= ri, own_row, own_col)
    put_mask(4, cr > ri, own_row, doc(base - NB + (cr >> 5)))
    put_mask(5, cr <= ri, own_row, doc(base + (cr >> 5)))
    flip = jnp.where(ri + ci == LANES - 1, 1.0, 0.0).astype(jnp.bfloat16)

    def keep(b):
        blk = base + b
        start = (blk == 0) | (blk == ends[0]) | (blk == ends[1]) | (blk == ends[2])
        return jnp.where(start, 0.0, 1.0).astype(jnp.float32)

    loads[0].wait()
    part = jnp.zeros((ROWS, LANES), jnp.float32)
    for t in range(4):
        ut = raw[3, :, t * LANES:(t + 1) * LANES].astype(jnp.float32)
        part = part + ut * ut
    row = jnp.sum(part.T, axis=0, keepdims=True)
    loads[4].wait()
    lift = rewb[...].astype(jnp.float32) * 0.25
    xs[0:1] = row
    xs[1:2] = lift
    xs[2:8] = jnp.zeros((6, LANES), jnp.float32)

    for c in (loads[1], loads[2], loads[3], loads[5], loads[6]):
        c.wait()

    def extend(i, b, before):
        ext[i, b, 0:8] = before * keep(b)
        ext[i, b, 8:40] = raw[i, b * BLK:(b + 1) * BLK].astype(jnp.float32)

    def filtered(i, b):
        w = seb[i].astype(jnp.float32)
        acc = w[0:1] * ext[i, b, 8:40]
        for j in range(1, TAPS):
            acc = acc + w[j:j + 1] * ext[i, b, 8 - j:40 - j]
        return acc

    def block(b):
        rows = pl.ds(b * BLK, BLK)
        qs = filtered(0, b)
        uq = qs * raw[3, rows].astype(jnp.float32)
        uqf[rows] = uq
        uqb[rows] = uq.astype(jnp.bfloat16)
        ks = filtered(1, b)
        vs = filtered(2, b)
        short[0, rows] = ks
        short[1, rows] = vs
        zown[rows] = (ks * vs).astype(jnp.bfloat16)

    for b in range(1, NB):
        for i in range(3):
            extend(i, b, raw[i, b * BLK - 16:b * BLK].astype(jnp.float32)[8:16])
        block(b)

    pl.semaphore_wait(barrier, len(peers))

    tail = pl.ds(BLK, ROWS - BLK)
    head = pl.ds(0, BLK)
    x_copies = [send(xs, xr.at[o - 1], X0 + o - 1, x_peer(o)) for o in range(1, NX)]
    rims = [send(raw.at[i, pl.ds(ROWS - 16, 16)], rim.at[i], RIM0 + i, (nxt, f)) for i in range(3)]
    z_tail = send(zown.at[tail], zprev.at[tail], ZH0, (nxt, f))
    u_tail = send(uqb.at[tail], uqn.at[tail], UH0, (prv, f))
    for c in x_copies + rims + [z_tail, u_tail]:
        c.start()

    taps = mrb[...]
    back = jnp.dot(taps, jnp.where(lax.rem(ri + ci, LANES) == 0, 1.0, 0.0).astype(jnp.bfloat16),
                   preferred_element_type=jnp.float32)
    skew[0, 0:GRP] = taps.astype(jnp.float32)
    skew[1, 0:GRP] = back

    def build(g, c):
        fr = jnp.broadcast_to(skew[1, pl.ds(g, 1)], (ROWS, LANES))
        cf = pltpu.roll(fr, 0, axis=1, stride=1, stride_axis=0)
        tf[g, :, 0:LANES] = (cf * mask[0]).astype(jnp.bfloat16)
        tf[g, :, LANES:2 * LANES] = (cf * mask[1]).astype(jnp.bfloat16)
        br = jnp.broadcast_to(skew[0, pl.ds(g, 1)], (ROWS, LANES))
        cb = pltpu.roll(br, 0, axis=1, stride=1, stride_axis=0)
        tb[g, :, 0:LANES] = (cb * mask[3]).astype(jnp.bfloat16)
        tb[g, :, LANES:2 * LANES] = (cb * mask[2]).astype(jnp.bfloat16)
        return c

    lax.fori_loop(0, GRP, build, 0)

    for c in x_copies:
        c.wait_recv()
    zs[...] = xs[...] + xr[0] + xr[1] + xr[2]
    zs[1:2] = lift
    z_copies = [
        send(zs, zr.at[0], ZP0, (d, fz)),
        send(zs, zr.at[1], ZP0 + 1, (prv, f)),
        send(zs, zr.at[2], ZP0 + 2, (prv, fz)),
    ]
    for c in z_copies:
        c.start()

    for c in rims:
        c.wait_recv()
    for i in range(3):
        extend(i, 0, rim[i].astype(jnp.float32)[8:16])
    block(0)
    z_head = send(zown.at[head], zprev.at[head], ZH0 + 1, (nxt, f))
    u_head = send(uqb.at[head], uqn.at[head], UH0 + 1, (prv, f))
    z_head.start()
    u_head.start()
    z_tail.wait_recv()
    z_head.wait_recv()

    lane_grp = ci >> 4

    for t in range(4):
        lanes = slice(t * LANES, (t + 1) * LANES)
        zp, zo = zprev[:, lanes], zown[:, lanes]
        zc = jnp.concatenate([zp, zo], axis=0)
        zrp = jnp.dot(flip, zp, preferred_element_type=jnp.float32).astype(jnp.bfloat16)
        zro = jnp.dot(flip, zo, preferred_element_type=jnp.float32).astype(jnp.bfloat16)
        zrc = jnp.concatenate([zrp, zro], axis=0)
        ub = uqb[:, lanes]
        med = jnp.zeros((ROWS, LANES), jnp.float32)
        for g in range(8):
            o = jnp.dot(tf[t * 8 + g], zc, preferred_element_type=jnp.float32)
            med = jnp.where(lane_grp == g, o, med)
            sel = jnp.where(lane_grp == g, ub, jnp.zeros_like(ub))
            a = lax.dot_general(sel, zrc, (((1,), (1,)), ((), ())), preferred_element_type=jnp.float32)
            cmix = a[:, 0:LANES] * mask[4] + a[:, LANES:2 * LANES] * mask[5]
            skew[t * 8 + g] = pltpu.roll(cmix, 1, axis=1, stride=1, stride_axis=0)
        umb[:, lanes] = med * raw[3, :, lanes].astype(jnp.float32)

    u_tail.wait_recv()
    u_head.wait_recv()
    for c in z_copies:
        c.wait_recv()
    tot_own = zs[0:1] + zr[0][0:1]
    tot_next = zr[1][0:1] + zr[2][0:1]
    s_own = lift * lax.rsqrt(tot_own / CH + 1e-06)
    s_next = zr[1][1:2] * lax.rsqrt(tot_next / CH + 1e-06)
    scol[...] = jnp.broadcast_to(s_own, (ROWS, LANES)).T
    s_next_col = jnp.broadcast_to(s_next, (ROWS, LANES)).T
    s_col = scol[...]
    for t in range(4):
        lanes = slice(t * LANES, (t + 1) * LANES)
        dmo[:, lanes] = (s_col * uqf[:, lanes]).astype(jnp.bfloat16)
        dmn[:, lanes] = (s_next_col * uqn[:, lanes].astype(jnp.float32)).astype(jnp.bfloat16)

    inv = 1.0 / ROWS

    def reduce_short(i, t, cot):
        lanes = slice(t * LANES, (t + 1) * LANES)
        acc = [jnp.zeros((8, LANES), jnp.float32) for _ in range(TAPS)]
        for b in range(NB):
            cb = cot[b * BLK:(b + 1) * BLK]
            for j in range(TAPS):
                pr = cb * ext[i, b, 8 - j:40 - j, lanes]
                acc[j] = acc[j] + jnp.sum(pr.reshape(4, 8, LANES), axis=0)
        for j in range(TAPS):
            pay[4 * i + t, j:j + 1] = jnp.sum(acc[j], axis=0, keepdims=True) * inv
        pay[4 * i + t, 7:8] = jnp.zeros((1, LANES), jnp.float32)

    for t in range(4):
        lanes = slice(t * LANES, (t + 1) * LANES)
        dc = jnp.concatenate([dmo[:, lanes], dmn[:, lanes]], axis=0)
        dz = jnp.zeros((ROWS, LANES), jnp.float32)
        for g in range(8):
            o = jnp.dot(tb[t * 8 + g], dc, preferred_element_type=jnp.float32)
            dz = jnp.where(lane_grp == g, o, dz)
        reduce_short(0, t, s_col * umb[:, lanes])
        reduce_short(1, t, dz * short[1, :, lanes])
        reduce_short(2, t, dz * short[0, :, lanes])

    for m in range(4):
        for r in range(8):
            pr = scol[...] * skew[m * 8 + r]
            pay[12 + m, r:r + 1] = jnp.sum(pr, axis=0, keepdims=True) * inv

    rs_copies = []
    for o in range(1, TEAM):
        to = lax.rem(me + o, TEAM)
        rs_copies.append(send(pay.at[to], rsb.at[o - 1], RS0 + o - 1, team_of(to)))
    for c in rs_copies:
        c.start()
    total = pay[me]
    for o in range(1, TEAM):
        rs_copies[o - 1].wait_recv()
        total = total + rsb[o - 1]
    zzb[zlo] = total
    zz_copies = [send(zzb.at[zlo], zzb.at[zlo], ZZ0 + o - 1, z_peer(o)) for o in range(1, NZ)]
    for c in zz_copies:
        c.start()
    for c in zz_copies:
        c.wait_recv()
    total = zzb[0]
    for i in range(1, NZ):
        total = total + zzb[i]
    fin[...] = total
    ag_copies = []
    for o in range(1, TEAM):
        ag_copies.append(send(fin, got.at[me], AG0 + o - 1, team_of(lax.rem(me + o, TEAM))))
    for c in ag_copies:
        c.start()
    got[me] = total
    for c in x_copies + rims + [z_tail, u_tail, z_head, u_head] + z_copies + rs_copies + zz_copies:
        c.wait_send()
    for c in ag_copies:
        c.wait_recv()
    out_ref[...] = got[...]
    for c in ag_copies:
        c.wait_send()


def split_kernel(x_ref, se_ref, mr_ref):
    for i in range(3):
        for t in range(4):
            se_ref[i, :, t * LANES:(t + 1) * LANES] = x_ref[4 * i + t, 0:TAPS]
    for m in range(4):
        mr_ref[m * 8:(m + 1) * 8] = x_ref[12 + m]


def on_device(query, key, value, upstream, reward, lengths, se_filter, mr_filter):
    f32, bf16 = jnp.float32, jnp.bfloat16
    vm = pltpu.VMEM
    anyspec = pl.BlockSpec(memory_space=pl.ANY)
    scratch = [
        vm((4, ROWS, COLS), bf16), vm((1, ROWS), jnp.int32), vm((3, TAPS, COLS), bf16), vm((GRP, LANES), bf16),
        vm((3, 16, COLS), bf16), vm((3, NB, 40, COLS), f32), vm((2, ROWS, COLS), f32),
        vm((ROWS, COLS), bf16), vm((ROWS, COLS), bf16), vm((ROWS, COLS), f32), vm((ROWS, COLS), bf16),
        vm((ROWS, COLS), bf16), vm((ROWS, COLS), f32), vm((6, ROWS, LANES), f32),
        vm((GRP, ROWS, 2 * LANES), bf16), vm((GRP, ROWS, 2 * LANES), bf16), vm((GRP, ROWS, LANES), f32),
        vm((8, LANES), f32), vm((3, 8, LANES), f32), vm((8, LANES), f32), vm((3, 8, LANES), f32),
        vm((ROWS, LANES), f32), vm((ROWS, COLS), bf16), vm((ROWS, COLS), bf16),
        vm((TEAM, 8, LANES), f32), vm((TEAM - 1, 8, LANES), f32), vm((NZ, 8, LANES), f32),
        vm((8, LANES), f32), vm((TEAM, 8, LANES), f32),
        pltpu.SemaphoreType.DMA((7,)), pltpu.SemaphoreType.DMA((NSEM,)), pltpu.SemaphoreType.DMA((NSEM,)),
    ]
    packed = pl.pallas_call(
        main_kernel,
        out_shape=jax.ShapeDtypeStruct((TEAM, 8, LANES), f32),
        in_specs=[anyspec] * 5 + [pl.BlockSpec(memory_space=pltpu.SMEM)] + [anyspec] * 2,
        out_specs=pl.BlockSpec(memory_space=pltpu.VMEM),
        scratch_shapes=scratch,
        compiler_params=pltpu.CompilerParams(
            collective_id=0, has_side_effects=True, vmem_limit_bytes=50 * 1024 * 1024
        ),
        name="hyena_grads",
    )(query, key, value, upstream, reward.reshape(1, ROWS), lengths, se_filter, mr_filter.T)
    grad_se, grad_mr = pl.pallas_call(
        split_kernel,
        out_shape=(
            jax.ShapeDtypeStruct((3, TAPS, COLS), f32),
            jax.ShapeDtypeStruct((GRP, LANES), f32),
        ),
        in_specs=[pl.BlockSpec(memory_space=pltpu.VMEM)],
        out_specs=(pl.BlockSpec(memory_space=pltpu.VMEM), pl.BlockSpec(memory_space=pltpu.VMEM)),
        name="hyena_split",
    )(packed)
    return grad_se, grad_mr.T


def solution(mesh):
    in_specs = (
        P("dp", "fsdp"), P("dp", "fsdp"), P("dp", "fsdp"), P("dp", "fsdp"),
        P("dp"), P(), P(None, None, "fsdp"), P(None, "fsdp"),
    )
    out_specs = (P(None, None, "fsdp"), P(None, "fsdp"))
    return jax.shard_map(
        on_device, mesh=mesh, in_specs=in_specs, out_specs=out_specs, check_vma=False
    )
```

```python
import jax
import jax.numpy as jnp
from jax import lax
from jax.experimental import pallas as pl
from jax.experimental.pallas import tpu as pltpu
from jax.sharding import PartitionSpec as P

MESH = pl.DeviceIdType.MESH
CH = 4096
ROWS = 128
COLS = 512
BLK = 32
HEAD = 16
NB = 4
TAPS = 7
GRP = 32
LANES = 128
NY, NZ, NX = 8, 6, 4
DP = 96
TEAM = 16

RIM0, ZH0, UH0, RS0, ZZ0, AG0, SO0, SN0, ECHO, NSEM = 0, 3, 5, 8, 23, 28, 43, 51, 59, 60
WIRE = jnp.float32


def main_kernel(
    q_hbm, k_hbm, v_hbm, u_hbm, rew_hbm, len_ref, se_hbm, mr_hbm, out_ref,
    raw, rewb, seb, mrb, rim, nxh, nxe, ext, short, zown, zprev, uqf, uqb, uqn, umb, mask, tf, tb, skew,
    xs, ro, rn, sbuf, scol, dmo, dmn, pay, payb, rsb, zzb, fin, got,
    lsem, ssem, rsem, hop,
):
    d = lax.axis_index("dp")
    f = lax.axis_index("fsdp")
    core = lax.rem(d, 2)
    zlo = lax.rem(d // 2, NZ)
    y = d // (2 * NZ)
    xx, zhi = f // 2, lax.rem(f, 2)
    nxt, prv = lax.rem(d + 1, DP), lax.rem(d + DP - 1, DP)
    me = y * 2 + core

    def team_of(i):
        return ((i // 2) * (2 * NZ) + zlo * 2 + lax.rem(i, 2), f)

    def z_peer(o):
        return (y * (2 * NZ) + lax.rem(zlo + o, NZ) * 2 + core, f)

    def y_near(o, c):
        return (lax.rem(y + o + NY, NY) * (2 * NZ) + zlo * 2 + c, f)

    def x_of(o):
        return lax.rem(xx + o, NX) * 2

    def tell(sem, devs):
        for dev in devs:
            pl.semaphore_signal(sem, inc=1, device_id=dev, device_id_type=MESH)

    barrier = pltpu.get_barrier_semaphore()
    near = [y_near(o, c) for o in (-1, 1) for c in (core, 1 - core)]
    near += [(d + 1 - 2 * core, f), (prv, f)]

    @pl.when(zhi == 0)
    def _():
        tell(barrier, [(d, x_of(o) + 1) for o in range(NX)] + [(nxt, x_of(o) + 1) for o in range(NX)])
        tell(barrier, [(d, x_of(o)) for o in range(1, NX)] + [(nxt, x_of(o)) for o in range(NX)])

    def tell_line(sem, o):
        @pl.when(zlo >= o)
        def _():
            tell(sem, [(d - 2 * o, f)])

        @pl.when(zlo + o < NZ)
        def _():
            tell(sem, [(d + 2 * o, f)])

    def line_count(o):
        return (zlo + NZ - o) // NZ + (2 * NZ - 1 - o - zlo) // NZ

    tell(barrier, near)
    tell_line(barrier, 1)

    def send(src, dst, idx, dev, ridx=None):
        return pltpu.make_async_remote_copy(
            src_ref=src, dst_ref=dst, send_sem=ssem.at[idx], recv_sem=rsem.at[idx if ridx is None else ridx],
            device_id=dev, device_id_type=MESH,
        )

    loads = [
        pltpu.make_async_copy(src, dst, lsem.at[i])
        for i, (src, dst) in enumerate([
            (u_hbm, raw.at[3]), (k_hbm, raw.at[1]), (v_hbm, raw.at[2]), (q_hbm, raw.at[0]),
            (rew_hbm, rewb), (se_hbm, seb), (mr_hbm, mrb),
        ])
    ]
    for c in loads:
        c.start()

    ends = [len_ref[0]]
    for i in range(1, 4):
        ends.append(ends[-1] + len_ref[i])
    base = d * NB

    def doc(b):
        n = jnp.zeros_like(b)
        for e in ends:
            n = n + (b >= e).astype(jnp.int32)
        return jnp.where(b < 0, -1, n)

    ri = lax.broadcasted_iota(jnp.int32, (ROWS, LANES), 0)
    ci = lax.broadcasted_iota(jnp.int32, (ROWS, LANES), 1)
    cr = (LANES - 1) - ci
    own_row = doc(base + (ri >> 5))
    own_col = doc(base + (ci >> 5))

    def put_mask(i, cond, a, b):
        mask[i] = jnp.where(cond & (a == b), 1.0, 0.0).astype(jnp.float32)

    put_mask(0, ci > ri, own_row, doc(base - NB + (ci >> 5)))
    put_mask(1, ci <= ri, own_row, own_col)
    put_mask(2, ci < ri, own_row, doc(base + NB + (ci >> 5)))
    put_mask(3, ci >= ri, own_row, own_col)
    put_mask(4, cr > ri, own_row, doc(base - NB + (cr >> 5)))
    put_mask(5, cr <= ri, own_row, doc(base + (cr >> 5)))
    flip = jnp.where(ri + ci == LANES - 1, 1.0, 0.0).astype(jnp.bfloat16)

    def keep(b):
        blk = base + b
        start = (blk == 0) | (blk == ends[0]) | (blk == ends[1]) | (blk == ends[2])
        return jnp.where(start, 0.0, 1.0).astype(jnp.float32)

    loads[0].wait()
    part = jnp.zeros((ROWS, LANES), jnp.float32)
    for t in range(4):
        ut = raw[3, :, t * LANES:(t + 1) * LANES].astype(jnp.float32)
        part = part + ut * ut
    row = jnp.sum(part.T, axis=0, keepdims=True)
    loads[4].wait()
    lift = rewb[...].astype(jnp.float32) * 0.25
    xs[0:1] = row
    xs[1:2] = lift

    def extend(i, b, before):
        ext[i, b, 0:8] = before * keep(b)
        ext[i, b, 8:40] = raw[i, b * BLK:(b + 1) * BLK].astype(jnp.float32)

    def filtered(i, b, n):
        w = seb[i].astype(jnp.float32)
        acc = w[0:1] * ext[i, b, 8:8 + n]
        for j in range(1, TAPS):
            acc = acc + w[j:j + 1] * ext[i, b, 8 - j:8 + n - j]
        return acc

    def block(b, n=BLK):
        rows = pl.ds(b * BLK, n)
        qs = filtered(0, b, n)
        uq = qs * raw[3, rows].astype(jnp.float32)
        uqf[rows] = uq
        uqb[rows] = uq.astype(jnp.bfloat16)
        ks = filtered(1, b, n)
        vs = filtered(2, b, n)
        short[0, rows] = ks
        short[1, rows] = vs
        zown[rows] = (ks * vs).astype(jnp.bfloat16)

    def late_blocks():
        for c in (loads[1], loads[2], loads[3], loads[5], loads[6]):
            c.wait()
        for b in range(1, NB):
            for i in range(3):
                extend(i, b, raw[i, b * BLK - 16:b * BLK].astype(jnp.float32)[8:16])
            block(b)
        for i in range(3):
            extend(i, 0, jnp.zeros((8, COLS), jnp.float32))
        block(0)

    pl.when(zhi == 0)(late_blocks)
    pl.semaphore_wait(barrier, 13 + zhi + line_count(1))

    tail = pl.ds(HEAD, ROWS - HEAD)
    head = pl.ds(0, HEAD)
    own_sums = [send(xs, ro.at[o * 2 + zhi], SO0 + o, (d, x_of(o)), SO0 + o * 2 + zhi) for o in range(NX)]
    next_sums = [send(xs, rn.at[o * 2 + zhi], SN0 + o, (prv, x_of(o)), SN0 + o * 2 + zhi) for o in range(NX)]

    @pl.when(zhi == 1)
    def _():
        own_sums[0].start()

    for c in own_sums[1:] + next_sums:
        c.start()
    rims = [send(raw.at[i, pl.ds(ROWS - 16, 16)], rim.at[i], RIM0 + i, (nxt, f)) for i in range(3)]
    z_tail = send(zown.at[tail], zprev.at[tail], ZH0, (nxt, f))
    u_tail = [
        send(uqb.at[tail], uqn.at[tail], UH0, (prv, f)),
        send(raw.at[0, head], nxh.at[0], UH0 + 1, (prv, f)),
        send(raw.at[3, head], nxh.at[1], UH0 + 2, (prv, f)),
    ]
    tell(hop.at[0], [y_near(-1, core), y_near(1, core)])
    tell_line(hop.at[1], 1)
    pl.when(zhi == 1)(late_blocks)
    for c in rims + [z_tail]:
        c.start()

    @pl.when(zhi == 0)
    def _():
        for c in u_tail:
            c.start()

    taps = mrb[...]
    back = jnp.dot(taps, jnp.where(lax.rem(ri + ci, LANES) == 0, 1.0, 0.0).astype(jnp.bfloat16),
                   preferred_element_type=jnp.float32)
    skew[0, 0:GRP] = taps.astype(jnp.float32)
    skew[1, 0:GRP] = back

    def build(g, c):
        fr = jnp.broadcast_to(skew[1, pl.ds(g, 1)], (ROWS, LANES))
        cf = pltpu.roll(fr, 0, axis=1, stride=1, stride_axis=0)
        tf[g, :, 0:LANES] = (cf * mask[0]).astype(jnp.bfloat16)
        tf[g, :, LANES:2 * LANES] = (cf * mask[1]).astype(jnp.bfloat16)
        br = jnp.broadcast_to(skew[0, pl.ds(g, 1)], (ROWS, LANES))
        cb = pltpu.roll(br, 0, axis=1, stride=1, stride_axis=0)
        tb[g, :, 0:LANES] = (cb * mask[3]).astype(jnp.bfloat16)
        tb[g, :, LANES:2 * LANES] = (cb * mask[2]).astype(jnp.bfloat16)
        return c

    lax.fori_loop(0, GRP, build, 0)

    pl.semaphore_wait(hop.at[0], 2)
    tell(hop.at[2], [y_near(-2, core), y_near(2, core)])
    pl.semaphore_wait(hop.at[1], line_count(1))
    tell_line(hop.at[3], 2)

    for c in rims:
        c.wait_recv()

    @pl.when(zhi == 1)
    def _():
        for c in u_tail:
            c.start()

    pl.semaphore_wait(hop.at[3], line_count(2))
    tell_line(hop.at[4], 1)
    for i in range(3):
        ext[i, 0, 0:8] = rim[i].astype(jnp.float32)[8:16] * keep(0)
    block(0, HEAD)
    z_head = send(zown.at[head], zprev.at[head], ZH0 + 1, (nxt, f))
    z_head.start()
    z_tail.wait_recv()
    z_head.wait_recv()

    lane_grp = ci >> 4

    for t in range(4):
        lanes = slice(t * LANES, (t + 1) * LANES)
        zp, zo = zprev[:, lanes], zown[:, lanes]
        zc = jnp.concatenate([zp, zo], axis=0)
        zrp = jnp.dot(flip, zp, preferred_element_type=jnp.float32).astype(jnp.bfloat16)
        zro = jnp.dot(flip, zo, preferred_element_type=jnp.float32).astype(jnp.bfloat16)
        zrc = jnp.concatenate([zrp, zro], axis=0)
        ub = uqb[:, lanes]
        med = jnp.zeros((ROWS, LANES), jnp.float32)
        for g in range(8):
            o = jnp.dot(tf[t * 8 + g], zc, preferred_element_type=jnp.float32)
            med = jnp.where(lane_grp == g, o, med)
            sel = jnp.where(lane_grp == g, ub, jnp.zeros_like(ub))
            a = lax.dot_general(sel, zrc, (((1,), (1,)), ((), ())), preferred_element_type=jnp.float32)
            cmix = a[:, 0:LANES] * mask[4] + a[:, LANES:2 * LANES] * mask[5]
            skew[t * 8 + g] = pltpu.roll(cmix, 1, axis=1, stride=1, stride_axis=0)
        umb[:, lanes] = med * raw[3, :, lanes].astype(jnp.float32)

    for c in u_tail:
        c.wait_recv()
    nxe[0:8] = raw[0, ROWS - 16:ROWS].astype(jnp.float32)[8:16] * keep(NB)
    nxe[8:24] = nxh[0].astype(jnp.float32)
    w0 = seb[0].astype(jnp.float32)
    qn = w0[0:1] * nxe[8:24]
    for j in range(1, TAPS):
        qn = qn + w0[j:j + 1] * nxe[8 - j:24 - j]
    uqn[head] = (qn * nxh[1].astype(jnp.float32)).astype(jnp.bfloat16)
    echo = send(sbuf, sbuf, ECHO, (d, xx * 2 + 1))

    @pl.when(zhi == 0)
    def _():
        tot_own = xs[0:1]
        tot_next = jnp.zeros((1, LANES), jnp.float32)
        for o in range(NX):
            for h in range(2):
                if o + h > 0:
                    send(xs, ro.at[o * 2 + h], SO0, (d, f), SO0 + o * 2 + h).wait_recv()
                    tot_own = tot_own + ro[o * 2 + h][0:1]
                send(xs, rn.at[o * 2 + h], SN0, (d, f), SN0 + o * 2 + h).wait_recv()
                tot_next = tot_next + rn[o * 2 + h][0:1]
        sbuf[0:1] = lift * lax.rsqrt(tot_own / CH + 1e-06)
        sbuf[1:2] = rn[0][1:2] * lax.rsqrt(tot_next / CH + 1e-06)
        echo.start()

    @pl.when(zhi == 1)
    def _():
        echo.wait_recv()

    s_own = sbuf[0:1]
    s_next = sbuf[1:2]
    scol[...] = jnp.broadcast_to(s_own, (ROWS, LANES)).T
    s_next_col = jnp.broadcast_to(s_next, (ROWS, LANES)).T
    s_col = scol[...]
    for t in range(4):
        lanes = slice(t * LANES, (t + 1) * LANES)
        dmo[:, lanes] = (s_col * uqf[:, lanes]).astype(jnp.bfloat16)
        dmn[:, lanes] = (s_next_col * uqn[:, lanes].astype(jnp.float32)).astype(jnp.bfloat16)

    inv = 1.0 / ROWS

    def reduce_short(i, t, cot):
        lanes = slice(t * LANES, (t + 1) * LANES)
        acc = [jnp.zeros((8, LANES), jnp.float32) for _ in range(TAPS)]
        for b in range(NB):
            cb = cot[b * BLK:(b + 1) * BLK]
            for j in range(TAPS):
                pr = cb * ext[i, b, 8 - j:40 - j, lanes]
                acc[j] = acc[j] + jnp.sum(pr.reshape(4, 8, LANES), axis=0)
        for j in range(TAPS):
            pay[4 * i + t, j:j + 1] = jnp.sum(acc[j], axis=0, keepdims=True) * inv
        pay[4 * i + t, 7:8] = jnp.zeros((1, LANES), jnp.float32)

    for t in range(4):
        lanes = slice(t * LANES, (t + 1) * LANES)
        dc = jnp.concatenate([dmo[:, lanes], dmn[:, lanes]], axis=0)
        dz = jnp.zeros((ROWS, LANES), jnp.float32)
        for g in range(8):
            o = jnp.dot(tb[t * 8 + g], dc, preferred_element_type=jnp.float32)
            dz = jnp.where(lane_grp == g, o, dz)
        reduce_short(0, t, s_col * umb[:, lanes])
        reduce_short(1, t, dz * short[1, :, lanes])
        reduce_short(2, t, dz * short[0, :, lanes])

    for m in range(4):
        for r in range(8):
            pr = scol[...] * skew[m * 8 + r]
            pay[12 + m, r:r + 1] = jnp.sum(pr, axis=0, keepdims=True) * inv

    pl.semaphore_wait(hop.at[2], 2)
    pl.semaphore_wait(hop.at[4], line_count(1))

    payb[...] = pay[...].astype(WIRE)
    rs_copies = []
    for o in range(1, TEAM):
        to = lax.rem(me + o, TEAM)
        rs_copies.append(send(payb.at[to], rsb.at[o - 1], RS0 + o - 1, team_of(to)))
    for c in rs_copies:
        c.start()
    total = pay[me]
    for o in range(1, TEAM):
        rs_copies[o - 1].wait_recv()
        total = total + rsb[o - 1].astype(jnp.float32)
    zzb[zlo] = total
    zz_copies = [send(zzb.at[zlo], zzb.at[zlo], ZZ0 + o - 1, z_peer(o)) for o in range(1, NZ)]
    for c in zz_copies:
        c.start()
    for c in zz_copies:
        c.wait_recv()
    total = zzb[0]
    for i in range(1, NZ):
        total = total + zzb[i]
    fin[...] = total.astype(WIRE)
    ag_copies = []
    for o in range(1, TEAM):
        ag_copies.append(send(fin, got.at[me], AG0 + o - 1, team_of(lax.rem(me + o, TEAM))))
    for c in ag_copies:
        c.start()
    got[me] = total.astype(WIRE)
    for c in own_sums[1:] + next_sums + rims + [z_tail, z_head] + u_tail + rs_copies + zz_copies:
        c.wait_send()
    pl.when(zhi == 0)(echo.wait_send)
    pl.when(zhi == 1)(own_sums[0].wait_send)
    for c in ag_copies:
        c.wait_recv()
    out_ref[...] = got[...].astype(jnp.float32)
    for c in ag_copies:
        c.wait_send()


def split_kernel(x_ref, se_ref, mr_ref):
    for i in range(3):
        for t in range(4):
            se_ref[i, :, t * LANES:(t + 1) * LANES] = x_ref[4 * i + t, 0:TAPS]
    for m in range(4):
        mr_ref[m * 8:(m + 1) * 8] = x_ref[12 + m]


def on_device(query, key, value, upstream, reward, lengths, se_filter, mr_filter):
    f32, bf16 = jnp.float32, jnp.bfloat16
    vm = pltpu.VMEM
    anyspec = pl.BlockSpec(memory_space=pltpu.HBM)
    scratch = [
        vm((4, ROWS, COLS), bf16), vm((1, ROWS), jnp.int32), vm((3, TAPS, COLS), bf16), vm((GRP, LANES), bf16),
        vm((3, 16, COLS), bf16), vm((2, HEAD, COLS), bf16), vm((24, COLS), f32), vm((3, NB, 40, COLS), f32), vm((2, ROWS, COLS), f32),
        vm((ROWS, COLS), bf16), vm((ROWS, COLS), bf16), vm((ROWS, COLS), f32), vm((ROWS, COLS), bf16),
        vm((ROWS, COLS), bf16), vm((ROWS, COLS), f32), vm((6, ROWS, LANES), f32),
        vm((GRP, ROWS, 2 * LANES), bf16), vm((GRP, ROWS, 2 * LANES), bf16), vm((GRP, ROWS, LANES), f32),
        vm((2, LANES), f32), vm((8, 2, LANES), f32), vm((8, 2, LANES), f32), vm((2, LANES), f32),
        vm((ROWS, LANES), f32), vm((ROWS, COLS), bf16), vm((ROWS, COLS), bf16),
        vm((TEAM, 8, LANES), f32), vm((TEAM, 8, LANES), WIRE), vm((TEAM - 1, 8, LANES), WIRE), vm((NZ, 8, LANES), f32),
        vm((8, LANES), WIRE), vm((TEAM, 8, LANES), WIRE),
        pltpu.SemaphoreType.DMA((7,)), pltpu.SemaphoreType.DMA((NSEM,)), pltpu.SemaphoreType.DMA((NSEM,)),
        pltpu.SemaphoreType.REGULAR((5,)),
    ]
    packed = pl.pallas_call(
        main_kernel,
        out_shape=jax.ShapeDtypeStruct((TEAM, 8, LANES), f32),
        in_specs=[anyspec] * 5 + [pl.BlockSpec(memory_space=pltpu.SMEM)] + [anyspec] * 2,
        out_specs=pl.BlockSpec(memory_space=pltpu.VMEM),
        scratch_shapes=scratch,
        compiler_params=pltpu.CompilerParams(
            collective_id=0, has_side_effects=True, vmem_limit_bytes=67043328
        ),
        name="hyena_grads",
    )(query, key, value, upstream, reward.reshape(1, ROWS), lengths, se_filter, mr_filter.T)
    grad_se, grad_mr = pl.pallas_call(
        split_kernel,
        out_shape=(
            jax.ShapeDtypeStruct((3, TAPS, COLS), f32),
            jax.ShapeDtypeStruct((GRP, LANES), f32),
        ),
        in_specs=[pl.BlockSpec(memory_space=pltpu.VMEM)],
        out_specs=(pl.BlockSpec(memory_space=pltpu.VMEM), pl.BlockSpec(memory_space=pltpu.VMEM)),
        name="hyena_split",
    )(packed)
    return grad_se, grad_mr.T


def solution(mesh):
    in_specs = (
        P("dp", "fsdp"), P("dp", "fsdp"), P("dp", "fsdp"), P("dp", "fsdp"),
        P("dp"), P(), P(None, None, "fsdp"), P(None, "fsdp"),
    )
    out_specs = (P(None, None, "fsdp"), P(None, "fsdp"))
    return jax.shard_map(
        on_device, mesh=mesh, in_specs=in_specs, out_specs=out_specs, check_vma=False
    )
```

```python
import jax
import jax.numpy as jnp
from jax import lax
from jax.experimental import pallas as pl
from jax.experimental.pallas import tpu as pltpu
from jax.sharding import PartitionSpec as P

MESH = pl.DeviceIdType.MESH
CH = 4096
ROWS = 128
COLS = 512
BLK = 32
HEAD = 16
NB = 4
TAPS = 7
GRP = 32
LANES = 128
NY, NZ, NX = 8, 6, 4
DP = 96
TEAM = 16

RIM0, ZH0, UH0, RS0, ZZ0, AG0, SO0, SN0, ECHO, NSEM = 0, 3, 5, 8, 23, 28, 43, 51, 59, 60
WIRE = jnp.float32
FAR = (8, 7, 9, 6, 10, 5, 11, 4, 12, 3, 13, 2, 14, 1, 15)


def main_kernel(
    q_hbm, k_hbm, v_hbm, u_hbm, rew_hbm, len_ref, se_hbm, mr_hbm, se_out, mr_out,
    raw, rewb, seb, mrb, rim, nxh, nxe, ext, short, zown, zprev, uqf, uqb, uqn, umb, mask, tf, tb, skew,
    xs, ro, rn, sbuf, scol, dmo, dmn, pay, payb, rsb, zzb, fin, got,
    lsem, ssem, rsem, hop,
):
    d = lax.axis_index("dp")
    f = lax.axis_index("fsdp")
    core = lax.rem(d, 2)
    zlo = lax.rem(d // 2, NZ)
    y = d // (2 * NZ)
    xx, zhi = f // 2, lax.rem(f, 2)
    nxt, prv = lax.rem(d + 1, DP), lax.rem(d + DP - 1, DP)
    me = y * 2 + core

    def team_of(i):
        return ((i // 2) * (2 * NZ) + zlo * 2 + lax.rem(i, 2), f)

    def z_peer(o):
        return (y * (2 * NZ) + lax.rem(zlo + o, NZ) * 2 + core, f)

    def y_near(o, c):
        return (lax.rem(y + o + NY, NY) * (2 * NZ) + zlo * 2 + c, f)

    def x_of(o):
        return lax.rem(xx + o, NX) * 2

    def tell(sem, devs):
        for dev in devs:
            pl.semaphore_signal(sem, inc=1, device_id=dev, device_id_type=MESH)

    barrier = pltpu.get_barrier_semaphore()
    near = [y_near(o, c) for o in (-1, 1) for c in (core, 1 - core)]
    near += [(d + 1 - 2 * core, f), (prv, f)]

    @pl.when(zhi == 0)
    def _():
        tell(barrier, [(d, x_of(o) + 1) for o in range(NX)] + [(nxt, x_of(o) + 1) for o in range(NX)])
        tell(barrier, [(d, x_of(o)) for o in range(1, NX)] + [(nxt, x_of(o)) for o in range(NX)])

    def tell_line(sem, o):
        @pl.when(zlo >= o)
        def _():
            tell(sem, [(d - 2 * o, f)])

        @pl.when(zlo + o < NZ)
        def _():
            tell(sem, [(d + 2 * o, f)])

    def line_count(o):
        return (zlo + NZ - o) // NZ + (2 * NZ - 1 - o - zlo) // NZ

    tell(barrier, near)
    tell_line(barrier, 1)

    def send(src, dst, idx, dev, ridx=None):
        return pltpu.make_async_remote_copy(
            src_ref=src, dst_ref=dst, send_sem=ssem.at[idx], recv_sem=rsem.at[idx if ridx is None else ridx],
            device_id=dev, device_id_type=MESH,
        )

    loads = [
        pltpu.make_async_copy(src, dst, lsem.at[i])
        for i, (src, dst) in enumerate([
            (u_hbm, raw.at[3]), (k_hbm, raw.at[1]), (v_hbm, raw.at[2]), (q_hbm, raw.at[0]),
            (rew_hbm, rewb), (se_hbm, seb), (mr_hbm, mrb),
        ])
    ]
    for c in loads:
        c.start()

    ends = [len_ref[0]]
    for i in range(1, 4):
        ends.append(ends[-1] + len_ref[i])
    base = d * NB

    def doc(b):
        n = jnp.zeros_like(b)
        for e in ends:
            n = n + (b >= e).astype(jnp.int32)
        return jnp.where(b < 0, -1, n)

    ri = lax.broadcasted_iota(jnp.int32, (ROWS, LANES), 0)
    ci = lax.broadcasted_iota(jnp.int32, (ROWS, LANES), 1)
    cr = (LANES - 1) - ci
    own_row = doc(base + (ri >> 5))
    own_col = doc(base + (ci >> 5))

    def put_mask(i, cond, a, b):
        mask[i] = jnp.where(cond & (a == b), 1.0, 0.0).astype(jnp.float32)

    put_mask(0, ci > ri, own_row, doc(base - NB + (ci >> 5)))
    put_mask(1, ci <= ri, own_row, own_col)
    put_mask(2, ci < ri, own_row, doc(base + NB + (ci >> 5)))
    put_mask(3, ci >= ri, own_row, own_col)
    put_mask(4, cr > ri, own_row, doc(base - NB + (cr >> 5)))
    put_mask(5, cr <= ri, own_row, doc(base + (cr >> 5)))
    flip = jnp.where(ri + ci == LANES - 1, 1.0, 0.0).astype(jnp.bfloat16)

    def keep(b):
        blk = base + b
        start = (blk == 0) | (blk == ends[0]) | (blk == ends[1]) | (blk == ends[2])
        return jnp.where(start, 0.0, 1.0).astype(jnp.float32)

    loads[0].wait()
    part = jnp.zeros((ROWS, LANES), jnp.float32)
    for t in range(4):
        ut = raw[3, :, t * LANES:(t + 1) * LANES].astype(jnp.float32)
        part = part + ut * ut
    row = jnp.sum(part.T, axis=0, keepdims=True)
    loads[4].wait()
    lift = rewb[...].astype(jnp.float32) * 0.25
    xs[0:1] = row
    xs[1:2] = lift

    def extend(i, b, before):
        ext[i, b, 0:8] = before * keep(b)
        ext[i, b, 8:40] = raw[i, b * BLK:(b + 1) * BLK].astype(jnp.float32)

    def filtered(i, b, n):
        w = seb[i].astype(jnp.float32)
        acc = w[0:1] * ext[i, b, 8:8 + n]
        for j in range(1, TAPS):
            acc = acc + w[j:j + 1] * ext[i, b, 8 - j:8 + n - j]
        return acc

    def block(b, n=BLK):
        rows = pl.ds(b * BLK, n)
        qs = filtered(0, b, n)
        uq = qs * raw[3, rows].astype(jnp.float32)
        uqf[rows] = uq
        uqb[rows] = uq.astype(jnp.bfloat16)
        ks = filtered(1, b, n)
        vs = filtered(2, b, n)
        short[0, rows] = ks
        short[1, rows] = vs
        zown[rows] = (ks * vs).astype(jnp.bfloat16)

    def late_blocks():
        for c in (loads[1], loads[2], loads[3], loads[5], loads[6]):
            c.wait()
        for b in range(1, NB):
            for i in range(3):
                extend(i, b, raw[i, b * BLK - 16:b * BLK].astype(jnp.float32)[8:16])
            block(b)
        for i in range(3):
            extend(i, 0, jnp.zeros((8, COLS), jnp.float32))
        block(0)

    pl.when(zhi == 0)(late_blocks)
    pl.semaphore_wait(barrier, 13 + zhi + line_count(1))

    tail = pl.ds(HEAD, ROWS - HEAD)
    head = pl.ds(0, HEAD)
    own_sums = [send(xs, ro.at[o * 2 + zhi], SO0 + o, (d, x_of(o)), SO0 + o * 2 + zhi) for o in range(NX)]
    next_sums = [send(xs, rn.at[o * 2 + zhi], SN0 + o, (prv, x_of(o)), SN0 + o * 2 + zhi) for o in range(NX)]

    @pl.when(zhi == 1)
    def _():
        own_sums[0].start()

    for o in (2, 1, 3):
        own_sums[o].start()
        next_sums[o].start()
    next_sums[0].start()
    rims = [send(raw.at[i, pl.ds(ROWS - 16, 16)], rim.at[i], RIM0 + i, (nxt, f)) for i in range(3)]
    z_tail = send(zown.at[tail], zprev.at[tail], ZH0, (nxt, f))
    u_tail = [
        send(uqb.at[tail], uqn.at[tail], UH0, (prv, f)),
        send(raw.at[0, head], nxh.at[0], UH0 + 1, (prv, f)),
        send(raw.at[3, head], nxh.at[1], UH0 + 2, (prv, f)),
    ]
    tell(hop.at[0], [y_near(-1, core), y_near(1, core)])
    tell_line(hop.at[1], 1)
    pl.when(zhi == 1)(late_blocks)
    for c in rims + [z_tail]:
        c.start()

    @pl.when(zhi == 0)
    def _():
        for c in u_tail:
            c.start()

    taps = mrb[...]
    back = jnp.dot(taps, jnp.where(lax.rem(ri + ci, LANES) == 0, 1.0, 0.0).astype(jnp.bfloat16),
                   preferred_element_type=jnp.float32)
    skew[0, 0:GRP] = taps.astype(jnp.float32)
    skew[1, 0:GRP] = back

    def build(g, c):
        fr = jnp.broadcast_to(skew[1, pl.ds(g, 1)], (ROWS, LANES))
        cf = pltpu.roll(fr, 0, axis=1, stride=1, stride_axis=0)
        tf[g, :, 0:LANES] = (cf * mask[0]).astype(jnp.bfloat16)
        tf[g, :, LANES:2 * LANES] = (cf * mask[1]).astype(jnp.bfloat16)
        br = jnp.broadcast_to(skew[0, pl.ds(g, 1)], (ROWS, LANES))
        cb = pltpu.roll(br, 0, axis=1, stride=1, stride_axis=0)
        tb[g, :, 0:LANES] = (cb * mask[3]).astype(jnp.bfloat16)
        tb[g, :, LANES:2 * LANES] = (cb * mask[2]).astype(jnp.bfloat16)
        return c

    lax.fori_loop(0, GRP, build, 0)

    pl.semaphore_wait(hop.at[0], 2)
    tell(hop.at[2], [y_near(-2, core), y_near(2, core)])
    pl.semaphore_wait(hop.at[1], line_count(1))
    tell_line(hop.at[3], 2)

    for c in rims:
        c.wait_recv()

    @pl.when(zhi == 1)
    def _():
        for c in u_tail:
            c.start()

    pl.semaphore_wait(hop.at[3], line_count(2))
    tell_line(hop.at[4], 1)
    for i in range(3):
        ext[i, 0, 0:8] = rim[i].astype(jnp.float32)[8:16] * keep(0)
    block(0, HEAD)
    z_head = send(zown.at[head], zprev.at[head], ZH0 + 1, (nxt, f))
    z_head.start()
    z_tail.wait_recv()
    z_head.wait_recv()

    lane_grp = ci >> 4

    for t in range(4):
        lanes = slice(t * LANES, (t + 1) * LANES)
        zp, zo = zprev[:, lanes], zown[:, lanes]
        zc = jnp.concatenate([zp, zo], axis=0)
        zrp = jnp.dot(flip, zp, preferred_element_type=jnp.float32).astype(jnp.bfloat16)
        zro = jnp.dot(flip, zo, preferred_element_type=jnp.float32).astype(jnp.bfloat16)
        zrc = jnp.concatenate([zrp, zro], axis=0)
        ub = uqb[:, lanes]
        med = jnp.zeros((ROWS, LANES), jnp.float32)
        for g in range(8):
            o = jnp.dot(tf[t * 8 + g], zc, preferred_element_type=jnp.float32)
            med = jnp.where(lane_grp == g, o, med)
            sel = jnp.where(lane_grp == g, ub, jnp.zeros_like(ub))
            a = lax.dot_general(sel, zrc, (((1,), (1,)), ((), ())), preferred_element_type=jnp.float32)
            cmix = a[:, 0:LANES] * mask[4] + a[:, LANES:2 * LANES] * mask[5]
            skew[t * 8 + g] = pltpu.roll(cmix, 1, axis=1, stride=1, stride_axis=0)
        umb[:, lanes] = med * raw[3, :, lanes].astype(jnp.float32)

    for c in u_tail:
        c.wait_recv()
    nxe[0:8] = raw[0, ROWS - 16:ROWS].astype(jnp.float32)[8:16] * keep(NB)
    nxe[8:24] = nxh[0].astype(jnp.float32)
    w0 = seb[0].astype(jnp.float32)
    qn = w0[0:1] * nxe[8:24]
    for j in range(1, TAPS):
        qn = qn + w0[j:j + 1] * nxe[8 - j:24 - j]
    uqn[head] = (qn * nxh[1].astype(jnp.float32)).astype(jnp.bfloat16)
    echo = send(sbuf, sbuf, ECHO, (d, xx * 2 + 1))

    @pl.when(zhi == 0)
    def _():
        tot_own = xs[0:1]
        tot_next = jnp.zeros((1, LANES), jnp.float32)
        for o in range(NX):
            for h in range(2):
                if o + h > 0:
                    send(xs, ro.at[o * 2 + h], SO0, (d, f), SO0 + o * 2 + h).wait_recv()
                    tot_own = tot_own + ro[o * 2 + h][0:1]
                send(xs, rn.at[o * 2 + h], SN0, (d, f), SN0 + o * 2 + h).wait_recv()
                tot_next = tot_next + rn[o * 2 + h][0:1]
        sbuf[0:1] = lift * lax.rsqrt(tot_own / CH + 1e-06)
        sbuf[1:2] = rn[0][1:2] * lax.rsqrt(tot_next / CH + 1e-06)
        echo.start()

    @pl.when(zhi == 1)
    def _():
        echo.wait_recv()

    s_own = sbuf[0:1]
    s_next = sbuf[1:2]
    scol[...] = jnp.broadcast_to(s_own, (ROWS, LANES)).T
    s_next_col = jnp.broadcast_to(s_next, (ROWS, LANES)).T
    s_col = scol[...]
    for t in range(4):
        lanes = slice(t * LANES, (t + 1) * LANES)
        dmo[:, lanes] = (s_col * uqf[:, lanes]).astype(jnp.bfloat16)
        dmn[:, lanes] = (s_next_col * uqn[:, lanes].astype(jnp.float32)).astype(jnp.bfloat16)

    inv = 1.0 / ROWS

    def reduce_short(i, t, cot):
        lanes = slice(t * LANES, (t + 1) * LANES)
        acc = [jnp.zeros((8, LANES), jnp.float32) for _ in range(TAPS)]
        for b in range(NB):
            cb = cot[b * BLK:(b + 1) * BLK]
            for j in range(TAPS):
                pr = cb * ext[i, b, 8 - j:40 - j, lanes]
                acc[j] = acc[j] + jnp.sum(pr.reshape(4, 8, LANES), axis=0)
        for j in range(TAPS):
            pay[4 * i + t, j:j + 1] = jnp.sum(acc[j], axis=0, keepdims=True) * inv
        pay[4 * i + t, 7:8] = jnp.zeros((1, LANES), jnp.float32)

    for t in range(4):
        lanes = slice(t * LANES, (t + 1) * LANES)
        dc = jnp.concatenate([dmo[:, lanes], dmn[:, lanes]], axis=0)
        dz = jnp.zeros((ROWS, LANES), jnp.float32)
        for g in range(8):
            o = jnp.dot(tb[t * 8 + g], dc, preferred_element_type=jnp.float32)
            dz = jnp.where(lane_grp == g, o, dz)
        reduce_short(0, t, s_col * umb[:, lanes])
        reduce_short(1, t, dz * short[1, :, lanes])
        reduce_short(2, t, dz * short[0, :, lanes])

    for m in range(4):
        for r in range(8):
            pr = scol[...] * skew[m * 8 + r]
            pay[12 + m, r:r + 1] = jnp.sum(pr, axis=0, keepdims=True) * inv

    pl.semaphore_wait(hop.at[2], 2)
    pl.semaphore_wait(hop.at[4], line_count(1))

    payb[...] = pay[...].astype(WIRE)
    rs_copies = []
    for o in range(1, TEAM):
        to = lax.rem(me + o, TEAM)
        rs_copies.append(send(payb.at[to], rsb.at[o - 1], RS0 + o - 1, team_of(to)))
    for o in FAR:
        rs_copies[o - 1].start()
    total = pay[me]
    for o in range(1, TEAM):
        rs_copies[o - 1].wait_recv()
        total = total + rsb[o - 1].astype(jnp.float32)
    zzb[zlo] = total
    zz_copies = [send(zzb.at[zlo], zzb.at[zlo], ZZ0 + o - 1, z_peer(o)) for o in range(1, NZ)]
    for c in zz_copies:
        c.start()
    for c in zz_copies:
        c.wait_recv()
    total = zzb[0]
    for i in range(1, NZ):
        total = total + zzb[i]
    fin[...] = total.astype(WIRE)
    ag_copies = []
    for o in range(1, TEAM):
        ag_copies.append(send(fin, got.at[me], AG0 + o - 1, team_of(lax.rem(me + o, TEAM))))
    for o in FAR:
        ag_copies[o - 1].start()
    got[me] = total.astype(WIRE)
    for c in own_sums[1:] + next_sums + rims + [z_tail, z_head] + u_tail + rs_copies + zz_copies:
        c.wait_send()
    pl.when(zhi == 0)(echo.wait_send)
    pl.when(zhi == 1)(own_sums[0].wait_send)
    for c in ag_copies:
        c.wait_recv()
    for i in range(3):
        for t in range(4):
            se_out[i, :, t * LANES:(t + 1) * LANES] = got[4 * i + t, 0:TAPS]
    for m in range(4):
        mr_out[m * 8:(m + 1) * 8] = got[12 + m]
    for c in ag_copies:
        c.wait_send()


def on_device(query, key, value, upstream, reward, lengths, se_filter, mr_filter):
    f32, bf16 = jnp.float32, jnp.bfloat16
    vm = pltpu.VMEM
    anyspec = pl.BlockSpec(memory_space=pltpu.HBM)
    scratch = [
        vm((4, ROWS, COLS), bf16), vm((1, ROWS), jnp.int32), vm((3, TAPS, COLS), bf16), vm((GRP, LANES), bf16),
        vm((3, 16, COLS), bf16), vm((2, HEAD, COLS), bf16), vm((24, COLS), f32), vm((3, NB, 40, COLS), f32), vm((2, ROWS, COLS), f32),
        vm((ROWS, COLS), bf16), vm((ROWS, COLS), bf16), vm((ROWS, COLS), f32), vm((ROWS, COLS), bf16),
        vm((ROWS, COLS), bf16), vm((ROWS, COLS), f32), vm((6, ROWS, LANES), f32),
        vm((GRP, ROWS, 2 * LANES), bf16), vm((GRP, ROWS, 2 * LANES), bf16), vm((GRP, ROWS, LANES), f32),
        vm((2, LANES), f32), vm((8, 2, LANES), f32), vm((8, 2, LANES), f32), vm((2, LANES), f32),
        vm((ROWS, LANES), f32), vm((ROWS, COLS), bf16), vm((ROWS, COLS), bf16),
        vm((TEAM, 8, LANES), f32), vm((TEAM, 8, LANES), WIRE), vm((TEAM - 1, 8, LANES), WIRE), vm((NZ, 8, LANES), f32),
        vm((8, LANES), WIRE), vm((TEAM, 8, LANES), WIRE),
        pltpu.SemaphoreType.DMA((7,)), pltpu.SemaphoreType.DMA((NSEM,)), pltpu.SemaphoreType.DMA((NSEM,)),
        pltpu.SemaphoreType.REGULAR((5,)),
    ]
    grad_se, grad_mr = pl.pallas_call(
        main_kernel,
        out_shape=(vm((3, TAPS, COLS), f32), vm((GRP, LANES), f32)),
        in_specs=[anyspec] * 5 + [pl.BlockSpec(memory_space=pltpu.SMEM)] + [anyspec] * 2,
        out_specs=(pl.BlockSpec(memory_space=pltpu.VMEM), pl.BlockSpec(memory_space=pltpu.VMEM)),
        scratch_shapes=scratch,
        compiler_params=pltpu.CompilerParams(
            collective_id=0, has_side_effects=True, vmem_limit_bytes=67043328 - 65536
        ),
        name="hyena_grads",
    )(query, key, value, upstream, reward.reshape(1, ROWS), lengths, se_filter, mr_filter.T)
    return grad_se, grad_mr.T


def solution(mesh):
    in_specs = (
        P("dp", "fsdp"), P("dp", "fsdp"), P("dp", "fsdp"), P("dp", "fsdp"),
        P("dp"), P(), P(None, None, "fsdp"), P(None, "fsdp"),
    )
    out_specs = (P(None, None, "fsdp"), P(None, "fsdp"))
    return jax.shard_map(
        on_device, mesh=mesh, in_specs=in_specs, out_specs=out_specs, check_vma=False
    )
```

```python
import jax
import jax.numpy as jnp
from jax import lax
from jax.experimental import pallas as pl
from jax.experimental.pallas import tpu as pltpu
from jax.sharding import PartitionSpec as P

MESH = pl.DeviceIdType.MESH
CH = 4096
ROWS = 128
COLS = 512
BLK = 32
HEAD = 16
NB = 4
TAPS = 7
GRP = 32
LANES = 128
NY, NZ, NX = 8, 6, 4
DP = 96
TEAM = 16

RIM0, ZH0, UH0, RS0, ZZ0, AG0, SO0, SN0, ECHO, NSEM = 0, 3, 5, 8, 23, 28, 43, 51, 59, 60
WIRE = jnp.float32
FAR = (8, 7, 9, 6, 10, 5, 11, 4, 12, 3, 13, 2, 14, 1, 15)


def main_kernel(
    q_hbm, k_hbm, v_hbm, u_hbm, rew_hbm, len_ref, se_hbm, mr_hbm, se_out, mr_out,
    raw, rewb, seb, mrb, rim, nxh, nxe, ext, short, zown, zprev, uqf, uqb, uqn, prod, mask, tf, tb, skew,
    xs, ro, rn, sbuf, scol, dmo, dmn, pay, payb, rsb, zzb, fin, got,
    lsem, ssem, rsem, hop,
):
    d = lax.axis_index("dp")
    f = lax.axis_index("fsdp")
    core = lax.rem(d, 2)
    zlo = lax.rem(d // 2, NZ)
    y = d // (2 * NZ)
    xx, zhi = f // 2, lax.rem(f, 2)
    nxt, prv = lax.rem(d + 1, DP), lax.rem(d + DP - 1, DP)
    me = y * 2 + core

    def team_of(i):
        return ((i // 2) * (2 * NZ) + zlo * 2 + lax.rem(i, 2), f)

    def z_peer(o):
        return (y * (2 * NZ) + lax.rem(zlo + o, NZ) * 2 + core, f)

    def y_near(o, c):
        return (lax.rem(y + o + NY, NY) * (2 * NZ) + zlo * 2 + c, f)

    def x_of(o):
        return lax.rem(xx + o, NX) * 2

    def tell(sem, devs):
        for dev in devs:
            pl.semaphore_signal(sem, inc=1, device_id=dev, device_id_type=MESH)

    barrier = pltpu.get_barrier_semaphore()
    near = [y_near(o, c) for o in (-1, 1) for c in (core, 1 - core)]
    near += [(d + 1 - 2 * core, f), (prv, f)]

    @pl.when(zhi == 0)
    def _():
        tell(barrier, [(d, x_of(o) + 1) for o in range(NX)] + [(nxt, x_of(o) + 1) for o in range(NX)])
        tell(barrier, [(d, x_of(o)) for o in range(1, NX)] + [(nxt, x_of(o)) for o in range(NX)])

    def tell_line(sem, o):
        @pl.when(zlo >= o)
        def _():
            tell(sem, [(d - 2 * o, f)])

        @pl.when(zlo + o < NZ)
        def _():
            tell(sem, [(d + 2 * o, f)])

    def line_count(o):
        return (zlo + NZ - o) // NZ + (2 * NZ - 1 - o - zlo) // NZ

    tell(barrier, near)
    tell_line(barrier, 1)

    def send(src, dst, idx, dev, ridx=None):
        return pltpu.make_async_remote_copy(
            src_ref=src, dst_ref=dst, send_sem=ssem.at[idx], recv_sem=rsem.at[idx if ridx is None else ridx],
            device_id=dev, device_id_type=MESH,
        )

    loads = [
        pltpu.make_async_copy(src, dst, lsem.at[i])
        for i, (src, dst) in enumerate([
            (u_hbm, raw.at[3]), (k_hbm, raw.at[1]), (v_hbm, raw.at[2]), (q_hbm, raw.at[0]),
            (rew_hbm, rewb), (se_hbm, seb), (mr_hbm, mrb),
        ])
    ]
    for c in loads:
        c.start()

    ends = [len_ref[0]]
    for i in range(1, 4):
        ends.append(ends[-1] + len_ref[i])
    base = d * NB

    def doc(b):
        n = jnp.zeros_like(b)
        for e in ends:
            n = n + (b >= e).astype(jnp.int32)
        return jnp.where(b < 0, -1, n)

    ri = lax.broadcasted_iota(jnp.int32, (ROWS, LANES), 0)
    ci = lax.broadcasted_iota(jnp.int32, (ROWS, LANES), 1)
    cr = (LANES - 1) - ci
    own_row = doc(base + (ri >> 5))
    own_col = doc(base + (ci >> 5))

    def put_mask(i, cond, a, b):
        mask[i] = jnp.where(cond & (a == b), 1.0, 0.0).astype(jnp.float32)

    put_mask(0, ci > ri, own_row, doc(base - NB + (ci >> 5)))
    put_mask(1, ci <= ri, own_row, own_col)
    put_mask(2, ci < ri, own_row, doc(base + NB + (ci >> 5)))
    put_mask(3, ci >= ri, own_row, own_col)
    put_mask(4, cr > ri, own_row, doc(base - NB + (cr >> 5)))
    put_mask(5, cr <= ri, own_row, doc(base + (cr >> 5)))
    flip = jnp.where(ri + ci == LANES - 1, 1.0, 0.0).astype(jnp.bfloat16)

    def keep(b):
        blk = base + b
        start = (blk == 0) | (blk == ends[0]) | (blk == ends[1]) | (blk == ends[2])
        return jnp.where(start, 0.0, 1.0).astype(jnp.float32)

    loads[0].wait()
    part = jnp.zeros((ROWS, LANES), jnp.float32)
    for t in range(4):
        ut = raw[3, :, t * LANES:(t + 1) * LANES].astype(jnp.float32)
        part = part + ut * ut
    row = jnp.sum(part.T, axis=0, keepdims=True)
    loads[4].wait()
    lift = rewb[...].astype(jnp.float32) * 0.25
    xs[0:1] = row
    xs[1:2] = lift

    def extend(i, b, before):
        ext[i, b, 0:8] = before * keep(b)
        ext[i, b, 8:40] = raw[i, b * BLK:(b + 1) * BLK].astype(jnp.float32)

    def filtered(i, b, n):
        w = seb[i].astype(jnp.float32)
        acc = w[0:1] * ext[i, b, 8:8 + n]
        for j in range(1, TAPS):
            acc = acc + w[j:j + 1] * ext[i, b, 8 - j:8 + n - j]
        return acc

    def block(b, n=BLK):
        rows = pl.ds(b * BLK, n)
        qs = filtered(0, b, n)
        uq = qs * raw[3, rows].astype(jnp.float32)
        uqf[rows] = uq
        uqb[rows] = uq.astype(jnp.bfloat16)
        ks = filtered(1, b, n)
        vs = filtered(2, b, n)
        short[0, rows] = ks
        short[1, rows] = vs
        zown[rows] = (ks * vs).astype(jnp.bfloat16)

    def late_blocks():
        for c in (loads[1], loads[2], loads[3], loads[5], loads[6]):
            c.wait()
        for b in range(1, NB):
            for i in range(3):
                extend(i, b, raw[i, b * BLK - 16:b * BLK].astype(jnp.float32)[8:16])
            block(b)
        for i in range(3):
            extend(i, 0, jnp.zeros((8, COLS), jnp.float32))
        block(0)

    pl.when(zhi == 0)(late_blocks)
    pl.semaphore_wait(barrier, 13 + zhi + line_count(1))

    tail = pl.ds(HEAD, ROWS - HEAD)
    head = pl.ds(0, HEAD)
    own_sums = [send(xs, ro.at[o * 2 + zhi], SO0 + o, (d, x_of(o)), SO0 + o * 2 + zhi) for o in range(NX)]
    next_sums = [send(xs, rn.at[o * 2 + zhi], SN0 + o, (prv, x_of(o)), SN0 + o * 2 + zhi) for o in range(NX)]

    for o in (2, 1, 3):
        own_sums[o].start()
        next_sums[o].start()
    next_sums[0].start()

    @pl.when(zhi == 1)
    def _():
        own_sums[0].start()

    rims = [send(raw.at[i, pl.ds(ROWS - 16, 16)], rim.at[i], RIM0 + i, (nxt, f)) for i in range(3)]
    z_tail = send(zown.at[tail], zprev.at[tail], ZH0, (nxt, f))
    u_tail = [
        send(uqb.at[tail], uqn.at[tail], UH0, (prv, f)),
        send(raw.at[0, head], nxh.at[0], UH0 + 1, (prv, f)),
        send(raw.at[3, head], nxh.at[1], UH0 + 2, (prv, f)),
    ]
    tell(hop.at[0], [y_near(-1, core), y_near(1, core)])
    tell_line(hop.at[1], 1)
    pl.when(zhi == 1)(late_blocks)
    for c in rims + [z_tail]:
        c.start()

    @pl.when(zhi == 0)
    def _():
        for c in u_tail:
            c.start()

    taps = mrb[...]
    back = jnp.dot(taps, jnp.where(lax.rem(ri + ci, LANES) == 0, 1.0, 0.0).astype(jnp.bfloat16),
                   preferred_element_type=jnp.float32)
    skew[0, 0:GRP] = taps.astype(jnp.float32)
    skew[1, 0:GRP] = back

    def build(g, c):
        fr = jnp.broadcast_to(skew[1, pl.ds(g, 1)], (ROWS, LANES))
        cf = pltpu.roll(fr, 0, axis=1, stride=1, stride_axis=0)
        tf[g, :, 0:LANES] = (cf * mask[0]).astype(jnp.bfloat16)
        tf[g, :, LANES:2 * LANES] = (cf * mask[1]).astype(jnp.bfloat16)
        br = jnp.broadcast_to(skew[0, pl.ds(g, 1)], (ROWS, LANES))
        cb = pltpu.roll(br, 0, axis=1, stride=1, stride_axis=0)
        tb[g, :, 0:LANES] = (cb * mask[3]).astype(jnp.bfloat16)
        tb[g, :, LANES:2 * LANES] = (cb * mask[2]).astype(jnp.bfloat16)
        return c

    lax.fori_loop(0, GRP, build, 0)

    pl.semaphore_wait(hop.at[0], 2)
    tell(hop.at[2], [y_near(-2, core), y_near(2, core)])
    pl.semaphore_wait(hop.at[1], line_count(1))
    tell_line(hop.at[3], 2)

    for c in rims:
        c.wait_recv()

    @pl.when(zhi == 1)
    def _():
        for c in u_tail:
            c.start()

    pl.semaphore_wait(hop.at[3], line_count(2))
    tell_line(hop.at[4], 1)
    for i in range(3):
        ext[i, 0, 0:8] = rim[i].astype(jnp.float32)[8:16] * keep(0)
    block(0, HEAD)
    z_head = send(zown.at[head], zprev.at[head], ZH0 + 1, (nxt, f))
    z_head.start()

    for b in range(NB):
        rows = pl.ds(b * BLK, BLK)
        ks, vs = short[0, rows], short[1, rows]
        for j in range(TAPS):
            prod[1, j, rows] = vs * ext[1, b, 8 - j:40 - j]
            prod[2, j, rows] = ks * ext[2, b, 8 - j:40 - j]
    z_tail.wait_recv()
    z_head.wait_recv()

    lane_grp = ci >> 4

    for t in range(4):
        lanes = slice(t * LANES, (t + 1) * LANES)
        zp, zo = zprev[:, lanes], zown[:, lanes]
        zc = jnp.concatenate([zp, zo], axis=0)
        zrp = jnp.dot(flip, zp, preferred_element_type=jnp.float32).astype(jnp.bfloat16)
        zro = jnp.dot(flip, zo, preferred_element_type=jnp.float32).astype(jnp.bfloat16)
        zrc = jnp.concatenate([zrp, zro], axis=0)
        ub = uqb[:, lanes]
        med = jnp.zeros((ROWS, LANES), jnp.float32)
        for g in range(8):
            o = jnp.dot(tf[t * 8 + g], zc, preferred_element_type=jnp.float32)
            med = jnp.where(lane_grp == g, o, med)
            sel = jnp.where(lane_grp == g, ub, jnp.zeros_like(ub))
            a = lax.dot_general(sel, zrc, (((1,), (1,)), ((), ())), preferred_element_type=jnp.float32)
            cmix = a[:, 0:LANES] * mask[4] + a[:, LANES:2 * LANES] * mask[5]
            skew[t * 8 + g] = pltpu.roll(cmix, 1, axis=1, stride=1, stride_axis=0)
        um = med * raw[3, :, lanes].astype(jnp.float32)
        for b in range(NB):
            rows = pl.ds(b * BLK, BLK)
            for j in range(TAPS):
                prod[0, j, rows, lanes] = um[b * BLK:(b + 1) * BLK] * ext[0, b, 8 - j:40 - j, lanes]

    for c in u_tail:
        c.wait_recv()
    nxe[0:8] = raw[0, ROWS - 16:ROWS].astype(jnp.float32)[8:16] * keep(NB)
    nxe[8:24] = nxh[0].astype(jnp.float32)
    w0 = seb[0].astype(jnp.float32)
    qn = w0[0:1] * nxe[8:24]
    for j in range(1, TAPS):
        qn = qn + w0[j:j + 1] * nxe[8 - j:24 - j]
    uqn[head] = (qn * nxh[1].astype(jnp.float32)).astype(jnp.bfloat16)
    echo = send(sbuf, sbuf, ECHO, (d, xx * 2 + 1))

    @pl.when(zhi == 0)
    def _():
        tot_own = xs[0:1]
        tot_next = jnp.zeros((1, LANES), jnp.float32)
        for o in range(NX):
            for h in range(2):
                if o + h > 0:
                    send(xs, ro.at[o * 2 + h], SO0, (d, f), SO0 + o * 2 + h).wait_recv()
                    tot_own = tot_own + ro[o * 2 + h][0:1]
                send(xs, rn.at[o * 2 + h], SN0, (d, f), SN0 + o * 2 + h).wait_recv()
                tot_next = tot_next + rn[o * 2 + h][0:1]
        sbuf[0:1] = lift * lax.rsqrt(tot_own / CH + 1e-06)
        sbuf[1:2] = rn[0][1:2] * lax.rsqrt(tot_next / CH + 1e-06)
        echo.start()

    @pl.when(zhi == 1)
    def _():
        echo.wait_recv()

    s_own = sbuf[0:1]
    s_next = sbuf[1:2]
    scol[...] = jnp.broadcast_to(s_own, (ROWS, LANES)).T
    s_next_col = jnp.broadcast_to(s_next, (ROWS, LANES)).T
    s_col = scol[...]
    for t in range(4):
        lanes = slice(t * LANES, (t + 1) * LANES)
        dmo[:, lanes] = (s_col * uqf[:, lanes]).astype(jnp.bfloat16)
        dmn[:, lanes] = (s_next_col * uqn[:, lanes].astype(jnp.float32)).astype(jnp.bfloat16)

    inv = 1.0 / ROWS

    def reduce_short(i, t, cot):
        lanes = slice(t * LANES, (t + 1) * LANES)
        for j in range(TAPS):
            pr = jnp.sum((cot * prod[i, j, :, lanes]).reshape(16, 8, LANES), axis=0)
            pay[4 * i + t, j:j + 1] = jnp.sum(pr, axis=0, keepdims=True) * inv
        pay[4 * i + t, 7:8] = jnp.zeros((1, LANES), jnp.float32)

    for t in range(4):
        lanes = slice(t * LANES, (t + 1) * LANES)
        dc = jnp.concatenate([dmo[:, lanes], dmn[:, lanes]], axis=0)
        dz = jnp.zeros((ROWS, LANES), jnp.float32)
        for g in range(8):
            o = jnp.dot(tb[t * 8 + g], dc, preferred_element_type=jnp.float32)
            dz = jnp.where(lane_grp == g, o, dz)
        for r in range(8):
            pr = jnp.sum((s_col * skew[t * 8 + r]).reshape(16, 8, LANES), axis=0)
            pay[12 + t, r:r + 1] = jnp.sum(pr, axis=0, keepdims=True) * inv
        reduce_short(0, t, s_col)
        reduce_short(1, t, dz)
        reduce_short(2, t, dz)

    pl.semaphore_wait(hop.at[2], 2)
    pl.semaphore_wait(hop.at[4], line_count(1))

    payb[...] = pay[...].astype(WIRE)
    rs_copies = []
    for o in range(1, TEAM):
        to = lax.rem(me + o, TEAM)
        rs_copies.append(send(payb.at[to], rsb.at[o - 1], RS0 + o - 1, team_of(to)))
    for o in FAR:
        rs_copies[o - 1].start()
    total = pay[me]
    for o in range(1, TEAM):
        rs_copies[o - 1].wait_recv()
        total = total + rsb[o - 1].astype(jnp.float32)
    zzb[zlo] = total
    zz_copies = [send(zzb.at[zlo], zzb.at[zlo], ZZ0 + o - 1, z_peer(o)) for o in range(1, NZ)]
    for c in zz_copies:
        c.start()
    for c in zz_copies:
        c.wait_recv()
    total = zzb[0]
    for i in range(1, NZ):
        total = total + zzb[i]
    fin[...] = total.astype(WIRE)
    ag_copies = []
    for o in range(1, TEAM):
        ag_copies.append(send(fin, got.at[me], AG0 + o - 1, team_of(lax.rem(me + o, TEAM))))
    for o in FAR:
        ag_copies[o - 1].start()
    got[me] = total.astype(WIRE)
    for c in own_sums[1:] + next_sums + rims + [z_tail, z_head] + u_tail + rs_copies + zz_copies:
        c.wait_send()
    pl.when(zhi == 0)(echo.wait_send)
    pl.when(zhi == 1)(own_sums[0].wait_send)
    for c in ag_copies:
        c.wait_recv()
    for i in range(3):
        for t in range(4):
            se_out[i, :, t * LANES:(t + 1) * LANES] = got[4 * i + t, 0:TAPS]
    for m in range(4):
        mr_out[m * 8:(m + 1) * 8] = got[12 + m]
    for c in ag_copies:
        c.wait_send()


def on_device(query, key, value, upstream, reward, lengths, se_filter, mr_filter):
    f32, bf16 = jnp.float32, jnp.bfloat16
    vm = pltpu.VMEM
    anyspec = pl.BlockSpec(memory_space=pltpu.HBM)
    scratch = [
        vm((4, ROWS, COLS), bf16), vm((1, ROWS), jnp.int32), vm((3, TAPS, COLS), bf16), vm((GRP, LANES), bf16),
        vm((3, 16, COLS), bf16), vm((2, HEAD, COLS), bf16), vm((24, COLS), f32), vm((3, NB, 40, COLS), f32), vm((2, ROWS, COLS), f32),
        vm((ROWS, COLS), bf16), vm((ROWS, COLS), bf16), vm((ROWS, COLS), f32), vm((ROWS, COLS), bf16),
        vm((ROWS, COLS), bf16), vm((3, TAPS, ROWS, COLS), f32), vm((6, ROWS, LANES), f32),
        vm((GRP, ROWS, 2 * LANES), bf16), vm((GRP, ROWS, 2 * LANES), bf16), vm((GRP, ROWS, LANES), f32),
        vm((2, LANES), f32), vm((8, 2, LANES), f32), vm((8, 2, LANES), f32), vm((2, LANES), f32),
        vm((ROWS, LANES), f32), vm((ROWS, COLS), bf16), vm((ROWS, COLS), bf16),
        vm((TEAM, 8, LANES), f32), vm((TEAM, 8, LANES), WIRE), vm((TEAM - 1, 8, LANES), WIRE), vm((NZ, 8, LANES), f32),
        vm((8, LANES), WIRE), vm((TEAM, 8, LANES), WIRE),
        pltpu.SemaphoreType.DMA((7,)), pltpu.SemaphoreType.DMA((NSEM,)), pltpu.SemaphoreType.DMA((NSEM,)),
        pltpu.SemaphoreType.REGULAR((5,)),
    ]
    grad_se, grad_mr = pl.pallas_call(
        main_kernel,
        out_shape=(vm((3, TAPS, COLS), f32), vm((GRP, LANES), f32)),
        in_specs=[anyspec] * 5 + [pl.BlockSpec(memory_space=pltpu.SMEM)] + [anyspec] * 2,
        out_specs=(pl.BlockSpec(memory_space=pltpu.VMEM), pl.BlockSpec(memory_space=pltpu.VMEM)),
        scratch_shapes=scratch,
        compiler_params=pltpu.CompilerParams(
            collective_id=0, has_side_effects=True, vmem_limit_bytes=67043328 - 65536
        ),
        name="hyena_grads",
    )(query, key, value, upstream, reward.reshape(1, ROWS), lengths, se_filter, mr_filter.T)
    return grad_se, grad_mr.T


def solution(mesh):
    in_specs = (
        P("dp", "fsdp"), P("dp", "fsdp"), P("dp", "fsdp"), P("dp", "fsdp"),
        P("dp"), P(), P(None, None, "fsdp"), P(None, "fsdp"),
    )
    out_specs = (P(None, None, "fsdp"), P(None, "fsdp"))
    return jax.shard_map(
        on_device, mesh=mesh, in_specs=in_specs, out_specs=out_specs, check_vma=False
    )
```

```python
import jax
import jax.numpy as jnp
from jax import lax
from jax.experimental import pallas as pl
from jax.experimental.pallas import tpu as pltpu
from jax.sharding import PartitionSpec as P

MESH = pl.DeviceIdType.MESH
CH = 4096
ROWS = 128
COLS = 512
BLK = 32
HEAD = 16
NB = 4
TAPS = 7
GRP = 32
LANES = 128
NY, NZ, NX = 8, 6, 4
DP = 96
TEAM = 16

RIM0, ZH0, UH0, RS0, ZZ0, AG0, SO0, SN0, ECHO, NSEM = 0, 3, 5, 8, 23, 28, 43, 51, 59, 60
WIRE = jnp.float32
FAR = (8, 7, 9, 6, 10, 5, 11, 4, 12, 3, 13, 2, 14, 1, 15)


def main_kernel(
    q_hbm, k_hbm, v_hbm, u_hbm, rew_hbm, len_ref, se_hbm, mr_hbm, se_out, mr_out,
    raw, rewb, seb, mrb, rim, nxh, nxe, ext, short, zown, zprev, uqf, uqb, uqn, prod, mask, wmask, tf, tb, skew,
    xs, ro, rn, sbuf, scol, dmo, dmn, pay, rsb, zzb, fin, got,
    lsem, ssem, rsem, hop,
):
    d = lax.axis_index("dp")
    f = lax.axis_index("fsdp")
    core = lax.rem(d, 2)
    zlo = lax.rem(d // 2, NZ)
    y = d // (2 * NZ)
    xx, zhi = f // 2, lax.rem(f, 2)
    nxt, prv = lax.rem(d + 1, DP), lax.rem(d + DP - 1, DP)
    me = y * 2 + core

    def team_of(i):
        return ((i // 2) * (2 * NZ) + zlo * 2 + lax.rem(i, 2), f)

    def z_peer(o):
        return (y * (2 * NZ) + lax.rem(zlo + o, NZ) * 2 + core, f)

    def y_near(o, c):
        return (lax.rem(y + o + NY, NY) * (2 * NZ) + zlo * 2 + c, f)

    def x_of(o):
        return lax.rem(xx + o, NX) * 2

    def tell(sem, devs):
        for dev in devs:
            pl.semaphore_signal(sem, inc=1, device_id=dev, device_id_type=MESH)

    barrier = pltpu.get_barrier_semaphore()
    near = [y_near(o, c) for o in (-1, 1) for c in (core, 1 - core)]
    near += [(d + 1 - 2 * core, f), (prv, f)]

    @pl.when(zhi == 0)
    def _():
        tell(barrier, [(d, x_of(o) + 1) for o in range(NX)] + [(nxt, x_of(o) + 1) for o in range(NX)])
        tell(barrier, [(d, x_of(o)) for o in range(1, NX)] + [(nxt, x_of(o)) for o in range(NX)])

    def tell_line(sem, o):
        @pl.when(zlo >= o)
        def _():
            tell(sem, [(d - 2 * o, f)])

        @pl.when(zlo + o < NZ)
        def _():
            tell(sem, [(d + 2 * o, f)])

    def line_count(o):
        return (zlo + NZ - o) // NZ + (2 * NZ - 1 - o - zlo) // NZ

    tell(barrier, near)
    tell_line(barrier, 1)

    def send(src, dst, idx, dev, ridx=None):
        return pltpu.make_async_remote_copy(
            src_ref=src, dst_ref=dst, send_sem=ssem.at[idx], recv_sem=rsem.at[idx if ridx is None else ridx],
            device_id=dev, device_id_type=MESH,
        )

    loads = [
        pltpu.make_async_copy(src, dst, lsem.at[i])
        for i, (src, dst) in enumerate([
            (u_hbm, raw.at[3]), (k_hbm, raw.at[1]), (v_hbm, raw.at[2]), (q_hbm, raw.at[0]),
            (rew_hbm, rewb), (se_hbm, seb), (mr_hbm, mrb),
        ])
    ]
    for c in loads:
        c.start()

    ends = [len_ref[0]]
    for i in range(1, 4):
        ends.append(ends[-1] + len_ref[i])
    base = d * NB

    def doc(b):
        n = jnp.zeros_like(b)
        for e in ends:
            n = n + (b >= e).astype(jnp.int32)
        return jnp.where(b < 0, -1, n)

    ri = lax.broadcasted_iota(jnp.int32, (ROWS, LANES), 0)
    ci = lax.broadcasted_iota(jnp.int32, (ROWS, LANES), 1)
    cr = (LANES - 1) - ci
    own_row = doc(base + (ri >> 5))
    own_col = doc(base + (ci >> 5))

    def put_mask(i, cond, a, b):
        mask[i] = jnp.where(cond & (a == b), 1.0, 0.0).astype(jnp.float32)

    put_mask(0, ci > ri, own_row, doc(base - NB + (ci >> 5)))
    put_mask(1, ci <= ri, own_row, own_col)
    put_mask(2, cr > ri, own_row, doc(base - NB + (cr >> 5)))
    put_mask(3, cr <= ri, own_row, doc(base + (cr >> 5)))
    flip = jnp.where(ri + ci == LANES - 1, 1.0, 0.0).astype(jnp.bfloat16)

    def keep(b):
        blk = base + b
        start = (blk == 0) | (blk == ends[0]) | (blk == ends[1]) | (blk == ends[2])
        return jnp.where(start, 0.0, 1.0).astype(jnp.float32)

    loads[0].wait()
    part = jnp.zeros((ROWS, LANES), jnp.float32)
    for t in range(4):
        ut = raw[3, :, t * LANES:(t + 1) * LANES].astype(jnp.float32)
        part = part + ut * ut
    row = jnp.sum(part.T, axis=0, keepdims=True)
    loads[4].wait()
    lift = rewb[...].astype(jnp.float32) * 0.25
    xs[0:1] = row
    xs[1:2] = lift

    def extend(i, b, before):
        ext[i, b, 0:8] = before * keep(b)
        ext[i, b, 8:40] = raw[i, b * BLK:(b + 1) * BLK].astype(jnp.float32)

    def filtered(i, b, n):
        w = seb[i].astype(jnp.float32)
        acc = w[0:1] * ext[i, b, 8:8 + n]
        for j in range(1, TAPS):
            acc = acc + w[j:j + 1] * ext[i, b, 8 - j:8 + n - j]
        return acc

    def block(b, n=BLK):
        rows = pl.ds(b * BLK, n)
        qs = filtered(0, b, n)
        uq = qs * raw[3, rows].astype(jnp.float32)
        uqf[rows] = uq
        uqb[rows] = uq.astype(jnp.bfloat16)
        ks = filtered(1, b, n)
        vs = filtered(2, b, n)
        short[0, rows] = ks
        short[1, rows] = vs
        zown[rows] = (ks * vs).astype(jnp.bfloat16)

    def late_blocks():
        for c in (loads[1], loads[2], loads[3], loads[5], loads[6]):
            c.wait()
        for b in range(1, NB):
            for i in range(3):
                extend(i, b, raw[i, b * BLK - 16:b * BLK].astype(jnp.float32)[8:16])
            block(b)
        for i in range(3):
            extend(i, 0, jnp.zeros((8, COLS), jnp.float32))
        block(0)

    pl.when(zhi == 0)(late_blocks)
    pl.semaphore_wait(barrier, 13 + zhi + line_count(1))

    tail = pl.ds(HEAD, ROWS - HEAD)
    head = pl.ds(0, HEAD)
    own_sums = [send(xs, ro.at[o * 2 + zhi], SO0 + o, (d, x_of(o)), SO0 + o * 2 + zhi) for o in range(NX)]
    next_sums = [send(xs, rn.at[o * 2 + zhi], SN0 + o, (prv, x_of(o)), SN0 + o * 2 + zhi) for o in range(NX)]

    for o in (2, 1, 3):
        own_sums[o].start()
        next_sums[o].start()
    next_sums[0].start()

    @pl.when(zhi == 1)
    def _():
        own_sums[0].start()

    rims = [send(raw.at[i, pl.ds(ROWS - 16, 16)], rim.at[i], RIM0 + i, (nxt, f)) for i in range(3)]
    z_tail = send(zown.at[tail], zprev.at[tail], ZH0, (nxt, f))
    u_tail = [
        send(uqb.at[tail], uqn.at[tail], UH0, (prv, f)),
        send(raw.at[0, head], nxh.at[0], UH0 + 1, (prv, f)),
        send(raw.at[3, head], nxh.at[1], UH0 + 2, (prv, f)),
    ]
    tell(hop.at[0], [y_near(-1, core), y_near(1, core)])
    tell_line(hop.at[1], 1)
    pl.when(zhi == 1)(late_blocks)
    for c in rims + [z_tail]:
        c.start()

    @pl.when(zhi == 0)
    def _():
        for c in u_tail:
            c.start()

    taps = mrb[...]
    back = jnp.dot(taps, jnp.where(lax.rem(ri + ci, LANES) == 0, 1.0, 0.0).astype(jnp.bfloat16),
                   preferred_element_type=jnp.float32)
    skew[0, 0:GRP] = taps.astype(jnp.float32)
    skew[1, 0:GRP] = back

    bc, br_i = ci[0:BLK], ri[0:BLK]

    def doc_of(b):
        n = jnp.int32(0)
        for e in ends:
            n = n + jnp.where(b >= e, 1, 0)
        return n

    for n in range(NB):
        for i in range(1, 5):
            same = jnp.where(doc_of(base + n) == doc_of(base + n + i), 1.0, 0.0).astype(jnp.float32)
            wmask[n * 4 + i - 1] = (jnp.ones((BLK, LANES), jnp.float32) * same).astype(jnp.bfloat16)

    def build(g, c):
        fr = jnp.broadcast_to(skew[1, pl.ds(g, 1)], (ROWS, LANES))
        cf = pltpu.roll(fr, 0, axis=1, stride=1, stride_axis=0)
        tf[g, :, 0:LANES] = (cf * mask[0]).astype(jnp.bfloat16)
        tf[g, :, LANES:2 * LANES] = (cf * mask[1]).astype(jnp.bfloat16)
        br = jnp.broadcast_to(skew[0, pl.ds(g, 1)], (BLK, LANES))
        cb = pltpu.roll(br, 0, axis=1, stride=1, stride_axis=0)
        tb[g, :, 0:LANES] = jnp.where(bc >= br_i, cb, 0.0).astype(jnp.bfloat16)
        tb[g, :, LANES:2 * LANES] = jnp.where(bc < br_i, cb, 0.0).astype(jnp.bfloat16)
        return c

    lax.fori_loop(0, GRP, build, 0)

    pl.semaphore_wait(hop.at[0], 2)
    tell(hop.at[2], [y_near(-2, core), y_near(2, core)])
    pl.semaphore_wait(hop.at[1], line_count(1))
    tell_line(hop.at[3], 2)

    for c in rims:
        c.wait_recv()

    @pl.when(zhi == 1)
    def _():
        for c in u_tail:
            c.start()

    pl.semaphore_wait(hop.at[3], line_count(2))
    tell_line(hop.at[4], 1)
    for i in range(3):
        ext[i, 0, 0:8] = rim[i].astype(jnp.float32)[8:16] * keep(0)
    block(0, HEAD)
    z_head = send(zown.at[head], zprev.at[head], ZH0 + 1, (nxt, f))
    z_head.start()

    for b in range(NB):
        rows = pl.ds(b * BLK, BLK)
        ks, vs = short[0, rows], short[1, rows]
        for j in range(TAPS):
            prod[1, j, rows] = vs * ext[1, b, 8 - j:40 - j]
            prod[2, j, rows] = ks * ext[2, b, 8 - j:40 - j]
    z_tail.wait_recv()
    z_head.wait_recv()

    lane_grp = ci >> 4

    for t in range(4):
        lanes = slice(t * LANES, (t + 1) * LANES)
        zp, zo = zprev[:, lanes], zown[:, lanes]
        zc = jnp.concatenate([zp, zo], axis=0)
        zrp = jnp.dot(flip, zp, preferred_element_type=jnp.float32).astype(jnp.bfloat16)
        zro = jnp.dot(flip, zo, preferred_element_type=jnp.float32).astype(jnp.bfloat16)
        zrc = jnp.concatenate([zrp, zro], axis=0)
        ub = uqb[:, lanes]
        med = jnp.zeros((ROWS, LANES), jnp.float32)
        for g in range(8):
            o = jnp.dot(tf[t * 8 + g], zc, preferred_element_type=jnp.float32)
            med = jnp.where(lane_grp == g, o, med)
            sel = jnp.where(lane_grp == g, ub, jnp.zeros_like(ub))
            a = lax.dot_general(sel, zrc, (((1,), (1,)), ((), ())), preferred_element_type=jnp.float32)
            cmix = a[:, 0:LANES] * mask[2] + a[:, LANES:2 * LANES] * mask[3]
            skew[t * 8 + g] = pltpu.roll(cmix, 1, axis=1, stride=1, stride_axis=0)
        um = med * raw[3, :, lanes].astype(jnp.float32)
        for b in range(NB):
            rows = pl.ds(b * BLK, BLK)
            for j in range(TAPS):
                prod[0, j, rows, lanes] = um[b * BLK:(b + 1) * BLK] * ext[0, b, 8 - j:40 - j, lanes]

    for c in u_tail:
        c.wait_recv()
    nxe[0:8] = raw[0, ROWS - 16:ROWS].astype(jnp.float32)[8:16] * keep(NB)
    nxe[8:24] = nxh[0].astype(jnp.float32)
    w0 = seb[0].astype(jnp.float32)
    qn = w0[0:1] * nxe[8:24]
    for j in range(1, TAPS):
        qn = qn + w0[j:j + 1] * nxe[8 - j:24 - j]
    uqn[head] = (qn * nxh[1].astype(jnp.float32)).astype(jnp.bfloat16)
    echo = send(sbuf, sbuf, ECHO, (d, xx * 2 + 1))

    @pl.when(zhi == 0)
    def _():
        tot_own = xs[0:1]
        tot_next = jnp.zeros((1, LANES), jnp.float32)
        for o in range(NX):
            for h in range(2):
                if o + h > 0:
                    send(xs, ro.at[o * 2 + h], SO0, (d, f), SO0 + o * 2 + h).wait_recv()
                    tot_own = tot_own + ro[o * 2 + h][0:1]
                send(xs, rn.at[o * 2 + h], SN0, (d, f), SN0 + o * 2 + h).wait_recv()
                tot_next = tot_next + rn[o * 2 + h][0:1]
        sbuf[0:1] = lift * lax.rsqrt(tot_own / CH + 1e-06)
        sbuf[1:2] = rn[0][1:2] * lax.rsqrt(tot_next / CH + 1e-06)
        echo.start()

    @pl.when(zhi == 1)
    def _():
        echo.wait_recv()

    s_own = sbuf[0:1]
    s_next = sbuf[1:2]
    scol[...] = jnp.broadcast_to(s_own, (ROWS, LANES)).T
    s_next_col = jnp.broadcast_to(s_next, (ROWS, LANES)).T
    s_col = scol[...]
    for t in range(4):
        lanes = slice(t * LANES, (t + 1) * LANES)
        dmo[:, lanes] = (s_col * uqf[:, lanes]).astype(jnp.bfloat16)
        dmn[:, lanes] = (s_next_col * uqn[:, lanes].astype(jnp.float32)).astype(jnp.bfloat16)

    inv = 1.0 / ROWS

    def reduce_short(i, t, cot):
        lanes = slice(t * LANES, (t + 1) * LANES)
        for j in range(TAPS):
            pr = jnp.sum((cot * prod[i, j, :, lanes]).reshape(16, 8, LANES), axis=0)
            pay[4 * i + t, j:j + 1] = jnp.sum(pr, axis=0, keepdims=True) * inv
        pay[4 * i + t, 7:8] = jnp.zeros((1, LANES), jnp.float32)

    pl.semaphore_wait(hop.at[2], 2)
    pl.semaphore_wait(hop.at[4], line_count(1))

    def scatter(k):
        o = lax.rem(k - me + TEAM, TEAM)
        slot = lax.rem(o + TEAM - 2, TEAM - 1)
        c = send(pay.at[k], rsb.at[slot], RS0 + slot, team_of(jnp.int32(k)))
        pl.when(o > 0)(c.start)

    for t in range(4):
        for r in range(8):
            pr = jnp.sum((s_col * skew[t * 8 + r]).reshape(16, 8, LANES), axis=0)
            pay[12 + t, r:r + 1] = jnp.sum(pr, axis=0, keepdims=True) * inv
        reduce_short(0, t, s_col)
    for k in (0, 1, 2, 3, 12, 13, 14, 15):
        scatter(k)

    for t in range(4):
        lanes = slice(t * LANES, (t + 1) * LANES)
        cut = [dmo[m * BLK:(m + 1) * BLK, lanes] for m in range(NB)]
        cut += [dmn[m * BLK:(m + 1) * BLK, lanes] for m in range(NB)]
        win = []
        for n in range(NB):
            seen = [cut[n]] + [cut[n + i] * wmask[n * 4 + i - 1] for i in range(1, 5)]
            win.append(jnp.concatenate(seen + [jnp.zeros((3 * BLK, LANES), jnp.bfloat16)], axis=0))
        band = tb[t * 8:t * 8 + 8].reshape(8 * BLK, 2 * LANES)
        parts = []
        for h in range(2):
            o = jnp.dot(band, jnp.concatenate(win[2 * h:2 * h + 2], axis=1), preferred_element_type=jnp.float32)
            for e in range(2):
                dzn = jnp.zeros((BLK, LANES), jnp.float32)
                for g in range(8):
                    dzn = jnp.where(lane_grp[0:BLK] == g, o[g * BLK:(g + 1) * BLK, e * LANES:(e + 1) * LANES], dzn)
                parts.append(dzn)
        dz = jnp.concatenate(parts, axis=0)
        reduce_short(1, t, dz)
        reduce_short(2, t, dz)


    rs_copies = []
    for o in range(1, TEAM):
        to = lax.rem(me + o, TEAM)
        rs_copies.append(send(pay.at[to], rsb.at[o - 1], RS0 + o - 1, team_of(to)))
    for k in range(4, 12):
        scatter(k)
    total = pay[me]
    for o in range(1, TEAM):
        rs_copies[o - 1].wait_recv()
        total = total + rsb[o - 1].astype(jnp.float32)
    zzb[zlo] = total
    zz_copies = [send(zzb.at[zlo], zzb.at[zlo], ZZ0 + o - 1, z_peer(o)) for o in range(1, NZ)]
    for c in zz_copies:
        c.start()
    for c in zz_copies:
        c.wait_recv()
    total = zzb[0]
    for i in range(1, NZ):
        total = total + zzb[i]
    fin[...] = total.astype(WIRE)
    ag_copies = []
    for o in range(1, TEAM):
        ag_copies.append(send(fin, got.at[me], AG0 + o - 1, team_of(lax.rem(me + o, TEAM))))
    for o in FAR:
        ag_copies[o - 1].start()
    got[me] = total.astype(WIRE)
    for c in own_sums[1:] + next_sums + rims + [z_tail, z_head] + u_tail + rs_copies + zz_copies:
        c.wait_send()
    pl.when(zhi == 0)(echo.wait_send)
    pl.when(zhi == 1)(own_sums[0].wait_send)
    for c in ag_copies:
        c.wait_recv()
    for i in range(3):
        for t in range(4):
            se_out[i, :, t * LANES:(t + 1) * LANES] = got[4 * i + t, 0:TAPS]
    for m in range(4):
        mr_out[m * 8:(m + 1) * 8] = got[12 + m]
    for c in ag_copies:
        c.wait_send()


def on_device(query, key, value, upstream, reward, lengths, se_filter, mr_filter):
    f32, bf16 = jnp.float32, jnp.bfloat16
    vm = pltpu.VMEM
    anyspec = pl.BlockSpec(memory_space=pltpu.HBM)
    scratch = [
        vm((4, ROWS, COLS), bf16), vm((1, ROWS), jnp.int32), vm((3, TAPS, COLS), bf16), vm((GRP, LANES), bf16),
        vm((3, 16, COLS), bf16), vm((2, HEAD, COLS), bf16), vm((24, COLS), f32), vm((3, NB, 40, COLS), f32), vm((2, ROWS, COLS), f32),
        vm((ROWS, COLS), bf16), vm((ROWS, COLS), bf16), vm((ROWS, COLS), f32), vm((ROWS, COLS), bf16),
        vm((ROWS, COLS), bf16), vm((3, TAPS, ROWS, COLS), f32), vm((4, ROWS, LANES), f32), vm((16, BLK, LANES), bf16),
        vm((GRP, ROWS, 2 * LANES), bf16), vm((GRP, BLK, 2 * LANES), bf16), vm((GRP, ROWS, LANES), f32),
        vm((2, LANES), f32), vm((8, 2, LANES), f32), vm((8, 2, LANES), f32), vm((2, LANES), f32),
        vm((ROWS, LANES), f32), vm((ROWS, COLS), bf16), vm((ROWS, COLS), bf16),
        vm((TEAM, 8, LANES), f32), vm((TEAM - 1, 8, LANES), WIRE), vm((NZ, 8, LANES), f32),
        vm((8, LANES), WIRE), vm((TEAM, 8, LANES), WIRE),
        pltpu.SemaphoreType.DMA((7,)), pltpu.SemaphoreType.DMA((NSEM,)), pltpu.SemaphoreType.DMA((NSEM,)),
        pltpu.SemaphoreType.REGULAR((5,)),
    ]
    grad_se, grad_mr = pl.pallas_call(
        main_kernel,
        out_shape=(vm((3, TAPS, COLS), f32), vm((GRP, LANES), f32)),
        in_specs=[anyspec] * 5 + [pl.BlockSpec(memory_space=pltpu.SMEM)] + [anyspec] * 2,
        out_specs=(pl.BlockSpec(memory_space=pltpu.VMEM), pl.BlockSpec(memory_space=pltpu.VMEM)),
        scratch_shapes=scratch,
        compiler_params=pltpu.CompilerParams(
            collective_id=0, has_side_effects=True, vmem_limit_bytes=67043328 - 65536
        ),
        name="hyena_grads",
    )(query, key, value, upstream, reward.reshape(1, ROWS), lengths, se_filter, mr_filter.T)
    return grad_se, grad_mr.T


def solution(mesh):
    in_specs = (
        P("dp", "fsdp"), P("dp", "fsdp"), P("dp", "fsdp"), P("dp", "fsdp"),
        P("dp"), P(), P(None, None, "fsdp"), P(None, "fsdp"),
    )
    out_specs = (P(None, None, "fsdp"), P(None, "fsdp"))
    return jax.shard_map(
        on_device, mesh=mesh, in_specs=in_specs, out_specs=out_specs, check_vma=False
    )
```
